32 devices in a mesh: patch: 4 (over z), seg: 8 (over y, x, core).
Axes of the slice: x: 2, y: 2, z: 4, core: 2. Of those that a mesh axis runs over, the one named last changes fastest.
Arguments:
- slave_local: int32 [65536], P(('patch', 'seg')), may hold values from 0 to 511
- owner_route: int32 [65536, 1], P(('patch', 'seg')), may hold values from 0 to 31; in each aligned block of 2048 rows (0 to 2047, 2048 to 4095, ...) at most 128 rows name the same one
- master_local: int32 [65536], P(('patch', 'seg')), may hold values from 0 to 511
- quad_slave: float32 [65536, 2, 128], P(('patch', 'seg')), may hold values from -1 to 1
- quad_master: float32 [65536, 2, 128], P(('patch', 'seg')), may hold values from -1 to 1
- quad_weight: float32 [65536, 128], P(('patch', 'seg')), may hold values from 0.01 to 0.1
- slave_coords: float32 [3, 9, 16384], P(None, None, ('patch', 'seg')), may hold values from -6 to 6
- slave_disp: float32 [3, 9, 16384], P(None, None, ('patch', 'seg')), may hold values from -4 to 4
- slave_normals: float32 [3, 9, 16384], P(None, None, ('patch', 'seg')), may hold values from -6 to 6
- multipliers: float32 [3, 9, 16384], P(None, None, ('patch', 'seg')), may hold values from -6 to 6
- master_coords: float32 [3, 9, 16384], P(None, None, ('patch', 'seg')), may hold values from -6 to 6
- master_disp: float32 [3, 9, 16384], P(None, None, ('patch', 'seg')), may hold values from -4 to 4
Outputs:
- coupling: float32 [81, 65536], P(None, ('patch', 'seg'))
- weighted_gap: float32 [9, 16384], P(None, ('patch', 'seg'))
- slave_mass: float32 [81, 16384], P(None, ('patch', 'seg'))
- master_force: float32 [27, 16384], P(None, ('patch', 'seg'))
- master_mass: float32 [81, 16384], P(None, ('patch', 'seg'))
The draws below stay inside these ranges and needn't reach their ends.
Inputs may be any that keep to these rules, and one draw needn't show every extreme that they name: `owner_route`: among the pairs of one device, no owner is named by more than 128 pairs, a bound that some block reaches.
All inputs are finite; a program needn't handle non-finite values.
Results may differ from the reference program's by a relative error of at most 0.0003.
Values sent between devices are 32-bit elements; how exact they have to be, the bound alone decides.
No kernel may reach another device: no remote copies, remote signals or barrier semaphores. Data moves between devices by JAX's collectives and lax.ppermute only.
A program may use at most 256 MiB of HBM per device.

```python
import math
import jax
import jax.numpy as jnp
import numpy as np
from jax import lax

NODES = 9
QP = 128
PAIR_DEV = 2048
SEG_DEV = 512
CAP = 128
PAIRS = 65536
SEGS = 16384
DEVICES = 32


def touch_ends(entries, rng, least, high):
    spot = [jax.random.randint(jax.random.fold_in(rng, axis), (), 0, length) for axis, length in enumerate(entries.shape)]
    longest = entries.shape.index(max(entries.shape))
    neighbour = spot[:longest] + [(spot[longest] + 1) % entries.shape[longest]] + spot[longest + 1:]
    return entries.at[tuple(spot)].set(least).at[tuple(neighbour)].set(high)


def shard_levels(own_key, extent, pieces, low, top_value):
    def one(axis_at, shards_of):
        steps = jax.random.uniform(jax.random.fold_in(jax.random.fold_in(own_key, 6), axis_at), (shards_of,), jnp.float32, low / len(pieces), top_value / len(pieces))
        return jnp.repeat(jnp.exp(steps), extent[axis_at] // shards_of).reshape((-1,) + (1,) * (len(extent) - axis_at - 1))

    factor_of = one(*pieces[0])
    for cut in pieces[1:]:
        factor_of = factor_of * one(*cut)
    return factor_of


def routed_block(stream_key, own, number, rows, number_of, top, bound, lean):
    ranking = jax.random.permutation(stream_key, number_of)
    packed, common = load_shares(number_of, rows * top, bound, lean, True), load_shares(number_of, rows * top, bound, lean, False)
    places = jnp.arange(number_of)

    def named(tallies, offset_by):
        used = int((tallies > 0).sum())
        fixed = max(1, used // 4)
        passed = fixed + (places - fixed + offset_by * (used - fixed)) % max(1, number_of - fixed)
        return jnp.zeros((number_of,), jnp.int32).at[ranking[jnp.where(places < fixed, places, passed)]].set(jnp.asarray(tallies, jnp.int32))

    tallies = jnp.where(number % 4 == 0, named(packed, number // 4), named(common, number - number // 4 - 1))
    mixed = jax.random.permutation(jax.random.fold_in(own, 3), number_of)
    source_of, taker = mixed[0:number_of // 2 * 2:2], mixed[1:number_of // 2 * 2:2]
    slack = jnp.minimum(tallies[source_of] - 1, bound - tallies[taker]) // 2
    slack = jnp.where((source_of == ranking[0]) | (taker == ranking[0]) | (tallies[taker] == 0), 0, jnp.maximum(slack, 0))
    passed = jax.random.randint(jax.random.fold_in(own, 4), (number_of // 2,), 0, 1 << 20) % (slack + 1)
    tallies = tallies.at[source_of].add(-passed).at[taker].add(passed)
    labels = jnp.searchsorted(jnp.cumsum(tallies), jnp.arange(rows * top), side="right").astype(jnp.int32)
    listing = labels.reshape(top, rows).T
    listing = listing[jax.random.permutation(jax.random.fold_in(own, 1), rows)]
    offset_by = jax.random.randint(jax.random.fold_in(own, 2), (rows, 1), 0, top)
    return jnp.take_along_axis(listing, (jnp.arange(top)[None, :] + offset_by) % top, axis=1)


def load_shares(amount, total, bound, slope, full):
    loads = [(1 << 20) // math.isqrt(rank ** slope) + 1 for rank in range(1, amount + 1)]
    largest = bound if full else min(bound, max(-(-total // amount), total * loads[0] // sum(loads)))
    least = 1 if total - largest >= amount - 1 else 0
    holding, rest = [largest] + [least] * (amount - 1), total - largest - least * (amount - 1)
    while rest > 0:
        candidates = [i for i in range(1, amount) if holding[i] < largest] or [i for i in range(1, amount) if holding[i] < bound]
        pool, left = sum([loads[i] for i in candidates]), rest
        for i in candidates:
            extra = min(bound - holding[i], max(1, left * loads[i] // pool), rest)
            holding[i] = holding[i] + extra
            rest = rest - extra
    return np.array(holding)


def normal_values(key, shape, scale, limit, cuts=(), kind=jnp.bfloat16):
    values = jax.random.normal(key, shape, jnp.float32) * scale
    if len(cuts) > 0:
        values = shard_levels(key, shape, cuts, -0.22, 0.18) * values
    return jnp.clip(values, min=-limit, max=limit).astype(kind)


def setup_inputs(seed: int = 0) -> dict:
    splits = jax.random.split(jax.random.key(seed), 13)
    slave_local = touch_ends(jax.random.randint(splits[0], (PAIRS,), 0, SEG_DEV), jax.random.fold_in(splits[0], 1), 0, SEG_DEV - 1).astype(jnp.int32)
    owner_route_keys = jax.random.split(jax.random.fold_in(splits[1], 1), PAIRS // PAIR_DEV)
    owner_route_turns = jax.random.permutation(jax.random.fold_in(splits[1], 3), PAIRS // PAIR_DEV)
    owner_route = jax.vmap(lambda own, number: routed_block(jax.random.fold_in(splits[1], 2), own, number, PAIR_DEV, DEVICES, 1, CAP, 2))(owner_route_keys, owner_route_turns).reshape((PAIRS, 1))
    master_local = touch_ends(jax.random.randint(splits[2], (PAIRS,), 0, SEG_DEV), jax.random.fold_in(splits[2], 1), 0, SEG_DEV - 1).astype(jnp.int32)
    quad_slave = jnp.clip(jax.random.uniform(splits[3], (PAIRS, 2, QP), jnp.float32, -1.0, 1.0) * shard_levels(splits[3], (PAIRS, 2, QP), ((0, 32),), -0.4, 0.0), -1.0, 1.0)
    quad_master = jnp.clip(jax.random.uniform(splits[4], (PAIRS, 2, QP), jnp.float32, -1.0, 1.0) * shard_levels(splits[4], (PAIRS, 2, QP), ((0, 32),), -0.4, 0.0), -1.0, 1.0)
    quad_weight = jnp.clip(jnp.exp(math.log(0.1) - 2.3025851 * jax.random.uniform(splits[5], (PAIRS, QP), jnp.float32) ** shard_levels(splits[5], (PAIRS, QP), ((0, 32),), -0.2, 0.2)), 0.01, 0.1)
    slave_coords = normal_values(splits[6], (3, NODES, SEGS), 1.0, 6.0, ((2, 32),), jnp.float32)
    slave_disp = normal_values(splits[7], (3, NODES, SEGS), 0.3, 4.0, ((2, 32),), jnp.float32)
    slave_normals = normal_values(splits[8], (3, NODES, SEGS), 0.6, 6.0, ((2, 32),), jnp.float32)
    multipliers = normal_values(splits[9], (3, NODES, SEGS), 1.0, 6.0, ((2, 32),), jnp.float32)
    master_coords = normal_values(splits[10], (3, NODES, SEGS), 1.0, 6.0, ((2, 32),), jnp.float32)
    master_disp = normal_values(splits[11], (3, NODES, SEGS), 0.3, 4.0, ((2, 32),), jnp.float32)
    return {"slave_local": slave_local, "owner_route": owner_route, "master_local": master_local, "quad_slave": quad_slave, "quad_master": quad_master, "quad_weight": quad_weight, "slave_coords": slave_coords, "slave_disp": slave_disp, "slave_normals": slave_normals, "multipliers": multipliers, "master_coords": master_coords, "master_disp": master_disp}


def lagrange_rows(t):
    return jnp.stack([0.5 * t * (t - 1.0), 1.0 - t * t, 0.5 * t * (t + 1.0)], axis=1)


def shape_values(points):
    first = lagrange_rows(points[:, 0, :])
    second = lagrange_rows(points[:, 1, :])
    product = second[:, :, None, :] * first[:, None, :, :]
    return product.reshape(points.shape[0], 9, points.shape[2])


def reference(slave_local, owner_route, master_local, quad_slave, quad_master, quad_weight, slave_coords, slave_disp, slave_normals, multipliers, master_coords, master_disp):
    highest = lax.Precision.HIGHEST
    slave_all = slave_coords + slave_disp
    master_all = master_coords + master_disp
    blocks = PAIRS // PAIR_DEV

    def one_block(carry, device):
        gap_sum, smass, mforce, mmass = carry
        start = (device * PAIR_DEV).astype(jnp.int32)
        local_slave = lax.dynamic_slice_in_dim(slave_local, start, PAIR_DEV)
        local_master = lax.dynamic_slice_in_dim(master_local, start, PAIR_DEV)
        owners = lax.dynamic_slice_in_dim(owner_route, start, PAIR_DEV)[:, 0]
        points_slave = lax.dynamic_slice_in_dim(quad_slave, start, PAIR_DEV)
        points_master = lax.dynamic_slice_in_dim(quad_master, start, PAIR_DEV)
        weights = lax.dynamic_slice_in_dim(quad_weight, start, PAIR_DEV)
        slave_index = (device * SEG_DEV + local_slave).astype(jnp.int32)
        master_index = (owners * SEG_DEV + local_master).astype(jnp.int32)
        slave_shape = shape_values(points_slave)
        master_shape = shape_values(points_master)
        weighted = slave_shape * weights[:, None, :]
        block_coupling = jnp.einsum("paq,pbq->abp", weighted, master_shape, precision=highest)
        slave_pos = jnp.take(slave_all, slave_index, axis=2)
        master_pos = jnp.take(master_all, master_index, axis=2)
        normals = jnp.take(slave_normals, slave_index, axis=2)
        lam = jnp.take(multipliers, slave_index, axis=2)
        slave_points = jnp.einsum("kap,paq->kpq", slave_pos, slave_shape, precision=highest)
        master_points = jnp.einsum("kap,paq->kpq", master_pos, master_shape, precision=highest)
        normal_points = jnp.einsum("kap,paq->kpq", normals, slave_shape, precision=highest)
        gap = jnp.sum(normal_points * (master_points - slave_points), axis=0)
        gap_terms = jnp.einsum("paq,pq->ap", weighted, gap, precision=highest)
        mass_terms = jnp.einsum("paq,pcq->acp", weighted, slave_shape, precision=highest).reshape(81, PAIR_DEV)
        force_terms = jnp.einsum("abp,kap->kbp", block_coupling, lam, precision=highest).reshape(27, PAIR_DEV)
        master_weighted = master_shape * weights[:, None, :]
        master_terms = jnp.einsum("pbq,pcq->bcp", master_weighted, master_shape, precision=highest).reshape(81, PAIR_DEV)
        carry = (gap_sum.at[:, slave_index].add(gap_terms), smass.at[:, slave_index].add(mass_terms),
                 mforce.at[:, master_index].add(force_terms), mmass.at[:, master_index].add(master_terms))
        return carry, block_coupling.reshape(81, PAIR_DEV)

    init = (jnp.zeros((9, SEGS), jnp.float32), jnp.zeros((81, SEGS), jnp.float32),
            jnp.zeros((27, SEGS), jnp.float32), jnp.zeros((81, SEGS), jnp.float32))
    carry, couplings = lax.scan(one_block, init, jnp.arange(blocks, dtype=jnp.int32))
    coupling = jnp.transpose(couplings, (1, 0, 2)).reshape(81, PAIRS)
    return (coupling, carry[0], carry[1], carry[2], carry[3])
```

```python
import functools

import jax
import jax.numpy as jnp
import numpy as np
from jax import lax
from jax.experimental import pallas as pl
from jax.experimental.pallas import tpu as pltpu
from jax.sharding import PartitionSpec as P

AXES = ("patch", "seg")
BLOCK = 128
F32 = jnp.float32
BF16 = jnp.bfloat16


def axis_products():
    axis = np.zeros((3, 3, 5), np.float32)
    axis[0, 0] = (1, 0, 0, -0.75, 0.25)
    axis[0, 1] = axis[1, 0] = (0, 0, 0, 1, 0)
    axis[0, 2] = axis[2, 0] = (0, 0, 0, -0.25, -0.25)
    axis[1, 1] = (0, 1, 0, -1, -1)
    axis[1, 2] = axis[2, 1] = (0, 0, 0, 0, 1)
    axis[2, 2] = (0, 0, 1, 0.25, -0.75)
    return axis


def reduced(x, along):
    x = np.moveaxis(x, along, 0)
    x = np.concatenate([x[1:2], x[0:1] - x[1:2], x[2:3] - x[1:2], x[3:]], axis=0)
    return np.moveaxis(x, 0, along)


def extra_moments():
    return [(m, n) for m in (3, 4) for n in range(5)] + [(m, n) for m in range(3) for n in (3, 4)]


def expansion(plain):
    axis = axis_products()
    table = np.zeros((81, 32), np.float32)
    for b in range(9):
        for c in range(9):
            both = np.einsum("m,n->mn", axis[b % 3, c % 3], axis[b // 3, c // 3])
            mixed = reduced(reduced(both, 0), 1)
            base = both if plain else mixed
            for n in range(3):
                for m in range(3):
                    table[9 * b + c, 3 * n + m] = base[m, n]
            for at, (m, n) in enumerate(extra_moments()):
                table[9 * b + c, 9 + at] = mixed[m, n]
    return table


def basis(t):
    square = t * t
    low = 0.5 * (square - t)
    middle = 1.0 - square
    high = low + t
    return [low, middle, high, low * middle, middle * high]


def reduced_rows(x):
    def along(at, stride):
        out = [None] * 9
        for q in range(3):
            low, middle, high = (at[q * (4 - stride) + stride * i] for i in range(3))
            for i, block in enumerate((middle, low - middle, high - middle)):
                out[q * (4 - stride) + stride * i] = block
        return out

    return along(along(x, 1), 3)


def split2(x):
    high = x.astype(BF16)
    low = (x - high.astype(F32)).astype(BF16)
    return high, low


def stack2(x):
    high = x.astype(BF16).astype(F32)
    return jnp.concatenate([high, x - high], axis=0).astype(BF16)


def dot(a, b):
    return jnp.dot(a, b, preferred_element_type=F32)


def dot_nt(a, b):
    return lax.dot_general(a, b, (((1,), (1,)), ((), ())), preferred_element_type=F32)


def joined(product):
    half = product.shape[0] // 2
    return product[:half] + product[half:]


def one_hot(index_row, rows):
    at = lax.broadcasted_iota(jnp.int32, (rows, index_row.shape[1]), 0)
    return jnp.where(at == index_row, 1.0, 0.0).astype(BF16)


def total(x):
    return jnp.sum(x, axis=0, keepdims=True)


def planes(ref):
    return ref[pl.ds(0, BLOCK, stride=2), :].T, ref[pl.ds(1, BLOCK, stride=2), :].T


def product(*factors):
    value = None
    for x in factors:
        if x is not None:
            value = x if value is None else value * x
    return value


def extra_rows(w, first, second):
    first = [None, first[0], first[2], first[3], first[4]]
    second = [None, second[0], second[2], second[3], second[4]]
    weighted = [product(w, x) for x in first]
    return [total(product(weighted[m], second[n])) for m, n in extra_moments()]


def fill_rows(table_ref, start, blocks):
    half = table_ref.shape[0] // 2
    for a, block in enumerate(blocks):
        high, low = split2(block)
        at = start + 3 * a
        table_ref[at : at + 3, :] = high
        table_ref[at + half : at + half + 3, :] = low


def terms_kernel(qs_ref, qm_ref, w_ref, sl_ref, ml_ref, lam_ref, *rest):
    coupling_ref, terms_ref, planes_ref, shape_ref, c_ref, lam_table_ref = rest[-6:]
    segments = lam_ref.shape[2]

    @pl.when(pl.program_id(0) == 0)
    def _():
        fill_rows(lam_table_ref, 0, [lam_ref[a] for a in range(9)])

    w = w_ref[...].T
    s, t = planes(qs_ref)
    u, v = planes(qm_ref)
    for at, plane in enumerate((s, t, u, v, w)):
        planes_ref[at] = plane
    fs, ft, fu, fv = basis(s)[:3], basis(t)[:3], basis(u), basis(v)
    for b in range(9):
        shape_ref[b] = fu[b % 3] * fv[b // 3]
    base = None
    for a in range(9):
        weighted = (w * fs[a % 3]) * ft[a // 3]
        for b in range(9):
            c_ref[a, b : b + 1, :] = total(weighted * shape_ref[b])
    lam = joined(dot(lam_table_ref[...], one_hot(sl_ref[...], segments)))
    for k in range(3):
        force = c_ref[0, 0:9, :] * lam[k : k + 1, :]
        for a in range(1, 9):
            force = force + c_ref[a, 0:9, :] * lam[3 * a + k : 3 * a + k + 1, :]
        terms_ref[9 * k : 9 * k + 9, :] = force
    base = c_ref[0, 0:9, :]
    coupling_ref[0:9, :] = base
    for a in range(1, 9):
        block = c_ref[a, 0:9, :]
        coupling_ref[9 * a : 9 * a + 9, :] = block
        base = base + block
    terms_ref[27:36, :] = base
    for at, row in enumerate(extra_rows(w, fu, fv)):
        terms_ref[36 + at : 37 + at, :] = row
    terms_ref[52:53, :] = ml_ref[...].astype(F32)
    terms_ref[53:56, :] = jnp.zeros((3, BLOCK), F32)


def slots_kernel(owner_ref, terms_ref, out_ref, left_ref, *, devices, cap):
    pairs = owner_ref.shape[1]
    width = 256
    per = width // cap
    groups = devices // per
    owner = owner_ref[...]
    upper = jnp.where(
        lax.broadcasted_iota(jnp.int32, (width, width), 0) < lax.broadcasted_iota(jnp.int32, (width, width), 1),
        1.0,
        0.0,
    ).astype(BF16)
    carry = jnp.zeros((devices, 1), F32)
    ranks = []
    for at in range(0, pairs, width):
        mine = one_hot(owner[:, at : at + width], devices)
        before = dot(mine, upper) + carry
        wide = mine.astype(F32)
        ranks.append(total(wide * before))
        carry = carry + jnp.sum(wide, axis=1, keepdims=True)
    rank = jnp.concatenate(ranks, axis=1).astype(jnp.int32)
    group = owner // per
    column = (owner - group * per) * cap + rank
    place = one_hot(column, width)
    both = stack2(terms_ref[...])
    rows = both.shape[0]
    for g in range(groups):
        left_ref[g * rows : (g + 1) * rows, :] = both * jnp.where(group == g, 1.0, 0.0).astype(BF16)
    sent = dot_nt(left_ref[...], place)
    for g in range(groups):
        block = joined(sent[g * rows : (g + 1) * rows])
        if cap == 128:
            out_ref[2 * g] = block[:, :128]
            out_ref[2 * g + 1] = block[:, 128:]
        else:
            out_ref[g] = block


def table_kernel(coords_ref, disp_ref, out_ref, rows_ref):
    rows_ref[...] = jnp.zeros_like(rows_ref)
    for i, block in enumerate(reduced_rows([coords_ref[a] + disp_ref[a] for a in range(9)])):
        for c in range(block.shape[1] // 128):
            at = 32 * c + 3 * i
            rows_ref[at : at + 3, :] = block[:, 128 * c : 128 * (c + 1)]
    out_ref[...] = rows_ref[...].T


def gap_kernel(
    row_ref, planes_ref, sl_ref, ml_ref, coords_ref, disp_ref, normals_ref, expand_ref, near_ref, far_ref,
    gap_ref, mass_ref, table_ref, slave_ref, sums_ref, a_ref, picked_ref, sems,
):
    segments = coords_ref.shape[2]
    step = pl.program_id(0)

    @pl.when(step == 0)
    def _():
        half = near_ref.shape[0]
        copies = [
            pltpu.make_async_copy(near_ref, table_ref.at[pl.ds(0, half)], sems.at[0]),
            pltpu.make_async_copy(far_ref, table_ref.at[pl.ds(half, half)], sems.at[1]),
        ]
        for copy in copies:
            copy.start()
        sums_ref[...] = jnp.zeros_like(sums_ref)
        a_ref[...] = jnp.zeros_like(a_ref)
        slave_ref[...] = jnp.zeros_like(slave_ref)
        fill_rows(slave_ref, 0, reduced_rows([coords_ref[a] + disp_ref[a] for a in range(9)]))
        fill_rows(slave_ref, 32, reduced_rows([normals_ref[a] for a in range(9)]))
        for copy in copies:
            copy.wait()

    hot_slave = one_hot(sl_ref[...], segments)
    slave = joined(dot(slave_ref[...], hot_slave))
    for p in range(BLOCK):
        picked_ref[p : p + 1, :] = table_ref[pl.ds(row_ref[step * BLOCK + p], 1), :]
    picked = picked_ref[...].T
    quarter = ml_ref[...] // 128
    position = picked[0:32]
    for c in range(1, segments // 128):
        position = jnp.where(quarter == c, picked[32 * c : 32 * c + 32], position)

    s, t, u, v, w = (planes_ref[at] for at in range(5))
    fs, ft = basis(s), basis(t)
    fu, fv = basis(u), basis(v)

    def field(coefs, row, first, second):
        value = None
        for j in range(3):
            c = [coefs[row + 9 * j + 3 * i : row + 9 * j + 3 * i + 1] for i in range(3)]
            part = c[0] + c[1] * first[0] + c[2] * first[2]
            value = part if j == 0 else value + part * second[0 if j == 1 else 2]
        return value

    gap = None
    for k in range(3):
        normal = field(slave, 32 + k, fs, ft)
        away = field(position, k, fu, fv) - field(slave, k, fs, ft)
        gap = normal * away if gap is None else gap + normal * away
    for n in range(3):
        for m in range(3):
            a = 3 * n + m
            weighted = product(w, (None, fs[0], fs[2])[m], (None, ft[0], ft[2])[n])
            a_ref[a : a + 1, :] = total(weighted)
            a_ref[32 + a : 33 + a, :] = total(weighted * gap)
    for at, row in enumerate(extra_rows(w, fs, ft)):
        a_ref[9 + at : 10 + at, :] = row
    sums_ref[...] += joined(dot_nt(stack2(a_ref[...]), hot_slave))

    @pl.when(step == pl.num_programs(0) - 1)
    def _():
        for j in range(3):
            for i in range(3):
                row = None
                for m, n, sign in lagrange_terms(i, j):
                    part = sums_ref[32 + 3 * n + m : 33 + 3 * n + m, :] * sign
                    row = part if row is None else row + part
                gap_ref[3 * j + i : 3 * j + i + 1, :] = row
        mass_ref[...] = expanded(expand_ref[...], sums_ref[0:32, :])


def lagrange_terms(i, j):
    axis = {0: [(1, 1.0)], 1: [(0, 1.0), (1, -1.0), (2, -1.0)], 2: [(2, 1.0)]}
    return [(m, n, p * q) for m, p in axis[i] for n, q in axis[j]]


def expanded(table, moments):
    high = moments.astype(BF16)
    rest = moments - high.astype(F32)
    middle = rest.astype(BF16)
    low = (rest - middle.astype(F32)).astype(BF16)
    return dot(table, high) + dot(table, middle) + dot(table, low)


def owner_kernel(in_ref, expand_ref, force_ref, mass_ref):
    chunks = in_ref.shape[0]
    segments = force_ref.shape[1]
    sums = jnp.zeros((2 * in_ref.shape[1], segments), F32)
    for at in range(0, chunks, 2):
        terms = jnp.concatenate([in_ref[at], in_ref[at + 1]], axis=1)
        hot = one_hot(terms[52:53, :].astype(jnp.int32), segments)
        sums = sums + dot_nt(stack2(terms), hot)
    sums = joined(sums)
    force_ref[...] = sums[0:27, :]
    moments = jnp.concatenate([sums[27:52, :], jnp.zeros((7, segments), F32)], axis=0)
    mass_ref[...] = expanded(expand_ref[...], moments)


def vmem(mib):
    return pltpu.CompilerParams(vmem_limit_bytes=mib << 20)


def from_patches(block):
    patches = lax.axis_size("patch")
    parts = [block]
    for d in range(1, patches):
        parts.append(lax.ppermute(block, "patch", [((i + d) % patches, i) for i in range(patches)]))
    return jnp.concatenate(parts, axis=0)


def from_chips(column):
    segs = lax.axis_size("seg")
    parts = [column]
    for d in range(1, segs // 2):
        parts.append(lax.ppermute(column, "seg", [(i ^ (2 * d), i) for i in range(segs)]))
    return jnp.concatenate(parts, axis=0)


def from_core(plane):
    return lax.ppermute(plane, "seg", [(i ^ 1, i) for i in range(lax.axis_size("seg"))])


def relative_owner(owner):
    patches, segs = lax.axis_size("patch"), lax.axis_size("seg")
    mine = lax.axis_index("seg")
    patch = jnp.mod(owner // segs - lax.axis_index("patch") + patches, patches)
    seg = jnp.bitwise_xor(owner % segs, mine)
    return (seg % 2) * (patches * segs // 2) + (seg // 2) * patches + patch


def shards(
    slave_local,
    owner_route,
    master_local,
    quad_slave,
    quad_master,
    quad_weight,
    slave_coords,
    slave_disp,
    slave_normals,
    multipliers,
    master_coords,
    master_disp,
):
    pairs = slave_local.shape[0]
    segments = slave_coords.shape[2]
    devices = lax.axis_size(AXES)
    cap = 2 * pairs // devices
    steps = pairs // BLOCK

    slave_coords, slave_disp, slave_normals, multipliers, master_coords, master_disp = (
        jnp.transpose(x, (1, 0, 2))
        for x in (slave_coords, slave_disp, slave_normals, multipliers, master_coords, master_disp)
    )
    block = pl.pallas_call(
        table_kernel,
        out_shape=jax.ShapeDtypeStruct((segments // 4, 128), F32),
        scratch_shapes=[pltpu.VMEM((128, segments // 4), F32)],
        name="table",
    )(master_coords, master_disp)
    column = from_patches(block)

    qs, qm, qw = (
        pltpu.with_memory_space_constraint(x, pltpu.HBM)
        for x in (quad_slave.reshape(2 * pairs, 128), quad_master.reshape(2 * pairs, 128), quad_weight)
    )
    sl = slave_local.reshape(1, pairs)
    ml = master_local.reshape(1, pairs)
    owner = owner_route.reshape(1, pairs)
    rows = relative_owner(owner_route.reshape(pairs)) * (segments // 4) + master_local % 128

    planes_spec = pl.BlockSpec((5, 128, BLOCK), lambda i: (0, 0, i))
    row_spec = pl.BlockSpec((1, BLOCK), lambda i: (0, i))

    def whole(x):
        return pl.BlockSpec(x.shape, lambda i: (0,) * len(x.shape))

    def terms_call(first, last, previous):

        def at(spec, dim):
            return pl.BlockSpec(spec, lambda i: tuple(i + first if d == dim else 0 for d in range(2)))

        weight = at((BLOCK, 128), 0)
        quad = at((2 * BLOCK, 128), 0)
        row = at((1, BLOCK), 1)
        return pl.pallas_call(
            terms_kernel,
            grid=(last - first,),
            in_specs=[quad, quad, weight, row, row, whole(multipliers)] + [pl.BlockSpec(memory_space=pl.ANY)] * len(previous),
            out_specs=[
                at((81, BLOCK), 1), at((56, BLOCK), 1), pl.BlockSpec((5, 128, BLOCK), lambda i: (0, 0, i + first)),
            ],
            out_shape=[jax.ShapeDtypeStruct(x, F32) for x in ((81, pairs), (56, pairs), (5, 128, pairs))],
            scratch_shapes=[
                pltpu.VMEM((9, 128, BLOCK), F32),
                pltpu.VMEM((9, 16, BLOCK), F32),
                pltpu.VMEM((64, segments), BF16),
            ],
            input_output_aliases={6 + i: i for i in range(len(previous))},
            compiler_params=vmem(40),
            cost_estimate=pl.CostEstimate(flops=10**9, transcendentals=0, bytes_accessed=15 * 10**6),
            name="terms",
        )(qs, qm, qw, sl, ml, multipliers, *previous)

    cuts = (0, 5 * steps // 16, 12 * steps // 16, steps)
    done = terms_call(cuts[0], cuts[1], ())
    column, done = lax.optimization_barrier((column, done))
    plane = from_chips(column)
    done = terms_call(cuts[1], cuts[2], done)
    plane, done = lax.optimization_barrier((plane, done))
    other = from_core(plane)
    done = terms_call(cuts[2], cuts[3], done)
    other, (coupling, terms, quads) = lax.optimization_barrier((other, done))

    shape = (devices, 56, 128) if cap == 128 else (devices * cap // 256, 56, 256)
    outgoing = pl.pallas_call(
        functools.partial(slots_kernel, devices=devices, cap=cap),
        out_shape=jax.ShapeDtypeStruct(shape, F32),
        scratch_shapes=[pltpu.VMEM((112 * devices * cap // 256, pairs), BF16)],
        compiler_params=vmem(48),
        name="slots",
    )(owner, terms)
    if cap != 128:
        outgoing = outgoing.reshape(shape[0], 56, 256 // cap, cap).transpose(0, 2, 1, 3).reshape(devices, 56, cap)
    incoming = lax.all_to_all(outgoing, AXES, split_axis=0, concat_axis=0, tiled=True)
    if cap != 128:
        incoming = (
            incoming.reshape(devices * cap // 128, 128 // cap, 56, cap).transpose(0, 2, 1, 3).reshape(-1, 56, 128)
        )

    expand = jnp.asarray(expansion(False), BF16)
    hbm = pl.BlockSpec(memory_space=pl.ANY)
    weighted_gap, slave_mass = pl.pallas_call(
        gap_kernel,
        grid=(steps,),
        in_specs=[
            pl.BlockSpec(memory_space=pltpu.SMEM), planes_spec, row_spec, row_spec,
            whole(slave_coords), whole(slave_disp), whole(slave_normals), whole(expand), hbm, hbm,
        ],
        out_specs=[pl.BlockSpec((9, segments), lambda i: (0, 0)), pl.BlockSpec((81, segments), lambda i: (0, 0))],
        out_shape=[jax.ShapeDtypeStruct((9, segments), F32), jax.ShapeDtypeStruct((81, segments), F32)],
        scratch_shapes=[
            pltpu.VMEM((devices * segments // 4, 128), F32),
            pltpu.VMEM((128, segments), BF16),
            pltpu.VMEM((48, segments), F32),
            pltpu.VMEM((48, BLOCK), F32),
            pltpu.VMEM((BLOCK, 128), F32),
            pltpu.SemaphoreType.DMA((2,)),
        ],
        compiler_params=vmem(56),
        cost_estimate=pl.CostEstimate(flops=2 * 10**9, transcendentals=0, bytes_accessed=30 * 10**6),
        name="gap",
    )(rows, quads, sl, ml, slave_coords, slave_disp, slave_normals, expand, plane, other)

    expand = jnp.asarray(expansion(True), BF16)
    force, master_mass = pl.pallas_call(
        owner_kernel,
        out_shape=[jax.ShapeDtypeStruct((27, segments), F32), jax.ShapeDtypeStruct((81, segments), F32)],
        compiler_params=vmem(40),
        name="owner",
    )(incoming, expand)
    return coupling, weighted_gap, slave_mass, force, master_mass


def solution(mesh):
    split = P(AXES)
    table = P(None, None, AXES)
    return jax.shard_map(
        shards,
        mesh=mesh,
        in_specs=(
            split, P(AXES, None), split, P(AXES, None, None), P(AXES, None, None), P(AXES, None),
            table, table, table, table, table, table,
        ),
        out_specs=(P(None, AXES),) * 5,
        check_vma=False,
    )
```

```python
import functools

import jax
import jax.numpy as jnp
import numpy as np
from jax import lax
from jax.experimental import pallas as pl
from jax.experimental.pallas import tpu as pltpu
from jax.sharding import PartitionSpec as P

AXES = ("patch", "seg")
BLOCK = 128
SUB = 2
UNROLL = (16, 16, 16)
F32 = jnp.float32
BF16 = jnp.bfloat16


def axis_products():
    axis = np.zeros((3, 3, 5), np.float32)
    axis[0, 0] = (1, 0, 0, -0.75, 0.25)
    axis[0, 1] = axis[1, 0] = (0, 0, 0, 1, 0)
    axis[0, 2] = axis[2, 0] = (0, 0, 0, -0.25, -0.25)
    axis[1, 1] = (0, 1, 0, -1, -1)
    axis[1, 2] = axis[2, 1] = (0, 0, 0, 0, 1)
    axis[2, 2] = (0, 0, 1, 0.25, -0.75)
    return axis


def reduced(x, along):
    x = np.moveaxis(x, along, 0)
    x = np.concatenate([x[1:2], x[0:1] - x[1:2], x[2:3] - x[1:2], x[3:]], axis=0)
    return np.moveaxis(x, 0, along)


def power_products():
    lagrange = np.array([(0, -0.5, 0.5), (1, 0, -1), (0, 0.5, 0.5)], np.float32)
    return np.array([[np.convolve(p, q) for q in lagrange] for p in lagrange], np.float32)


def extra_moments():
    return [(m, n) for m in (3, 4) for n in range(5)] + [(m, n) for m in range(3) for n in (3, 4)]


def expansion(powers):
    axis = power_products() if powers else axis_products()
    table = np.zeros((81, 32), np.float32)
    for b in range(9):
        for c in range(9):
            base = np.einsum("m,n->mn", axis[b % 3, c % 3], axis[b // 3, c // 3])
            mixed = base if powers else reduced(reduced(base, 0), 1)
            for n in range(3):
                for m in range(3):
                    table[9 * b + c, 3 * n + m] = base[m, n]
            for at, (m, n) in enumerate(extra_moments()):
                table[9 * b + c, 9 + at] = mixed[m, n]
    return table


def basis(t):
    square = t * t
    low = 0.5 * (square - t)
    middle = 1.0 - square
    high = low + t
    return [low, middle, high, low * middle, middle * high]


def powers(t):
    square = t * t
    return [None, t, square, square * t, square * square]


def power_rows(x):
    def along(at, stride):
        out = [None] * 9
        for q in range(3):
            low, middle, high = (at[q * (4 - stride) + stride * i] for i in range(3))
            for i, block in enumerate((middle, 0.5 * (high - low), 0.5 * (high + low) - middle)):
                out[q * (4 - stride) + stride * i] = block
        return out

    return along(along(x, 1), 3)


def split2(x):
    high = x.astype(BF16)
    low = (x - high.astype(F32)).astype(BF16)
    return high, low


def stack2(x):
    high = x.astype(BF16).astype(F32)
    return jnp.concatenate([high, x - high], axis=0).astype(BF16)


def dot(a, b):
    return jnp.dot(a, b, preferred_element_type=F32)


def dot_nt(a, b):
    return lax.dot_general(a, b, (((1,), (1,)), ((), ())), preferred_element_type=F32)


def joined(product):
    half = product.shape[0] // 2
    return product[:half] + product[half:]


def one_hot(index_row, rows):
    at = lax.broadcasted_iota(jnp.int32, (rows, index_row.shape[1]), 0)
    return jnp.where(at == index_row, 1.0, 0.0).astype(BF16)


def total(x):
    return jnp.sum(x, axis=0, keepdims=True)


def planes(ref, sub):
    at = 2 * BLOCK * sub
    return ref[pl.ds(at, BLOCK, stride=2), :].T, ref[pl.ds(at + 1, BLOCK, stride=2), :].T


def product(*factors):
    value = None
    for x in factors:
        if x is not None:
            value = x if value is None else value * x
    return value


def one_low_high(x):
    return [None, x[0], x[2], x[3], x[4]]


def extra_products(w, first, second):
    weighted = [product(w, x) for x in first]
    return [product(weighted[m], second[n]) for m, n in extra_moments()]


def accumulated(count, body, unroll):
    def step(c, sums):
        at = c * 8 if isinstance(c, int) else pl.multiple_of(c * 8, 8)
        return tuple(x + y for x, y in zip(sums, body(pl.ds(at, 8))))

    start = tuple(jnp.zeros((8, BLOCK), F32) for _ in range(count))
    return lax.fori_loop(0, 16, step, start, unroll=unroll)


def fill_rows(table_ref, start, blocks):
    half = table_ref.shape[0] // 2
    for a, block in enumerate(blocks):
        high, low = split2(block)
        at = start + 3 * a
        table_ref[at : at + 3, :] = high
        table_ref[at + half : at + half + 3, :] = low


def terms_kernel(qs_ref, qm_ref, w_ref, sl_ref, ml_ref, lam_ref, *rest):
    coupling_ref, terms_ref, planes_ref, shape_ref, c_ref, lam_table_ref = rest[-6:]
    segments = lam_ref.shape[2]

    @pl.when(pl.program_id(0) == 0)
    def _():
        fill_rows(lam_table_ref, 0, [lam_ref[a] for a in range(9)])

    for sub in range(SUB):
        terms_block(
            sub, qs_ref, qm_ref, w_ref, sl_ref, ml_ref, coupling_ref, terms_ref, planes_ref, shape_ref, c_ref,
            lam_table_ref, segments,
        )


def terms_block(
    sub, qs_ref, qm_ref, w_ref, sl_ref, ml_ref, coupling_ref, terms_ref, planes_ref, shape_ref, c_ref, lam_table_ref,
    segments,
):
    lanes = slice(sub * BLOCK, (sub + 1) * BLOCK)
    w = w_ref[lanes, :].T
    s, t = planes(qs_ref, sub)
    u, v = planes(qm_ref, sub)
    for at, plane in enumerate((s, t, u, v, w)):
        planes_ref[sub, at] = plane

    def prepared(rows):
        s, t, u, v, w = (planes_ref[sub, at, rows, :] for at in range(5))
        fs, ft, fu, fv = basis(s)[:3], basis(t)[:3], basis(u), basis(v)
        for j in range(3):
            for i in range(3):
                shape_ref[sub, 3 * j + i, rows, :] = fu[i] * fv[j]
                shape_ref[sub, 9 + 3 * j + i, rows, :] = (w * fs[i]) * ft[j]
        return extra_products(w, one_low_high(fu), one_low_high(fv))

    extras = accumulated(16, prepared, UNROLL[0])
    for j in range(3):

        def crossed(rows):
            master = [shape_ref[sub, b, rows, :] for b in range(9)]
            return [x * y for x in (shape_ref[sub, 9 + 3 * j + i, rows, :] for i in range(3)) for y in master]

        sums = accumulated(27, crossed, UNROLL[1])
        for i in range(3):
            for b in range(9):
                c_ref[sub, 3 * j + i, b : b + 1, :] = total(sums[9 * i + b])
    lam = joined(dot(lam_table_ref[...], one_hot(sl_ref[:, lanes], segments)))
    for k in range(3):
        force = c_ref[sub, 0, 0:9, :] * lam[k : k + 1, :]
        for a in range(1, 9):
            force = force + c_ref[sub, a, 0:9, :] * lam[3 * a + k : 3 * a + k + 1, :]
        terms_ref[9 * k : 9 * k + 9, lanes] = force
    base = c_ref[sub, 0, 0:9, :]
    coupling_ref[0:9, lanes] = base
    for a in range(1, 9):
        block = c_ref[sub, a, 0:9, :]
        coupling_ref[9 * a : 9 * a + 9, lanes] = block
        base = base + block
    terms_ref[27:36, lanes] = base
    for at, x in enumerate(extras):
        terms_ref[36 + at : 37 + at, lanes] = total(x)
    terms_ref[52:53, lanes] = ml_ref[:, lanes].astype(F32)
    terms_ref[53:56, lanes] = jnp.zeros((3, BLOCK), F32)


def slots_kernel(owner_ref, terms_ref, out_ref, left_ref, *, devices, cap):
    pairs = owner_ref.shape[1]
    width = 256
    per = width // cap
    groups = devices // per
    owner = owner_ref[...]
    upper = jnp.where(
        lax.broadcasted_iota(jnp.int32, (width, width), 0) < lax.broadcasted_iota(jnp.int32, (width, width), 1),
        1.0,
        0.0,
    ).astype(BF16)
    carry = jnp.zeros((devices, 1), F32)
    ranks = []
    for at in range(0, pairs, width):
        mine = one_hot(owner[:, at : at + width], devices)
        before = dot(mine, upper) + carry
        wide = mine.astype(F32)
        ranks.append(total(wide * before))
        carry = carry + jnp.sum(wide, axis=1, keepdims=True)
    rank = jnp.concatenate(ranks, axis=1).astype(jnp.int32)
    group = owner // per
    column = (owner - group * per) * cap + rank
    place = one_hot(column, width)
    both = stack2(terms_ref[...])
    rows = both.shape[0]
    for g in range(groups):
        left_ref[g * rows : (g + 1) * rows, :] = both * jnp.where(group == g, 1.0, 0.0).astype(BF16)
    sent = dot_nt(left_ref[...], place)
    for g in range(groups):
        block = joined(sent[g * rows : (g + 1) * rows])
        if cap == 128:
            out_ref[2 * g] = block[:, :128]
            out_ref[2 * g + 1] = block[:, 128:]
        else:
            out_ref[g] = block


def table_kernel(coords_ref, disp_ref, owner_ref, local_ref, out_ref, place_ref, rows_ref):
    place_ref[...] = relative_owner(owner_ref[...]) * out_ref.shape[0] + local_ref[...] % 128
    rows_ref[...] = jnp.zeros_like(rows_ref)
    for i, block in enumerate(power_rows([coords_ref[a] + disp_ref[a] for a in range(9)])):
        for c in range(block.shape[1] // 128):
            at = 32 * c + 3 * i
            rows_ref[at : at + 3, :] = block[:, 128 * c : 128 * (c + 1)]
    out_ref[...] = rows_ref[...].T


def gap_kernel(
    row_ref, planes_ref, sl_ref, ml_ref, coords_ref, disp_ref, normals_ref, expand_ref, near_ref, far_ref,
    gap_ref, mass_ref, table_ref, slave_ref, sums_ref, a_ref, picked_ref, coef_ref, wide_ref, hot_ref, sems,
):
    segments = coords_ref.shape[2]
    step = pl.program_id(0)

    @pl.when(step == 0)
    def _():
        half = near_ref.shape[0]
        copies = [
            pltpu.make_async_copy(near_ref, table_ref.at[pl.ds(0, half)], sems.at[0]),
            pltpu.make_async_copy(far_ref, table_ref.at[pl.ds(half, half)], sems.at[1]),
        ]
        for copy in copies:
            copy.start()
        a_ref[...] = jnp.zeros_like(a_ref)
        slave_ref[...] = jnp.zeros_like(slave_ref)
        fill_rows(slave_ref, 0, power_rows([coords_ref[a] + disp_ref[a] for a in range(9)]))
        fill_rows(slave_ref, 32, power_rows([normals_ref[a] for a in range(9)]))
        hot_ref[...] = one_hot(sl_ref[...], segments)
        coef_ref[0:64, :] = joined(dot(slave_ref[...], hot_ref[...]))
        for copy in copies:
            copy.wait()

    for sub in range(SUB):
        gap_block(sub, step, row_ref, ml_ref, planes_ref, table_ref, picked_ref, coef_ref, wide_ref, a_ref, segments)

    @pl.when(step == pl.num_programs(0) - 1)
    def _():
        sums_ref[...] = joined(dot_nt(stack2(a_ref[...]), hot_ref[...]))
        for j in range(3):
            for i in range(3):
                row = None
                for m, n, sign in lagrange_terms(i, j):
                    part = sums_ref[32 + 3 * n + m : 33 + 3 * n + m, :] * sign
                    row = part if row is None else row + part
                gap_ref[3 * j + i : 3 * j + i + 1, :] = row
        mass_ref[...] = expanded(expand_ref[...], sums_ref[0:32, :])


def gap_block(sub, step, row_ref, ml_ref, planes_ref, table_ref, picked_ref, coef_ref, wide_ref, a_ref, segments):
    start = pl.multiple_of((step * SUB + sub) * BLOCK, BLOCK)
    for p in range(BLOCK):
        picked_ref[sub, p : p + 1, :] = table_ref[pl.ds(row_ref[0, start + p], 1), :]
    picked = picked_ref[sub].T
    quarter = ml_ref[:, pl.ds(start, BLOCK)] // 128
    position = picked[0:32]
    for c in range(1, segments // 128):
        position = jnp.where(quarter == c, picked[32 * c : 32 * c + 32], position)
    here = pl.ds(start, BLOCK)
    for row in range(54):
        at = row if row < 27 else row + 5
        wide_ref[sub, row] = jnp.broadcast_to(coef_ref[at : at + 1, here], (8, BLOCK))
    for row in range(27):
        wide_ref[sub, 54 + row] = jnp.broadcast_to(position[row : row + 1], (8, BLOCK))

    def field(row, first, second):
        value = None
        for j in range(3):
            c = [wide_ref[sub, row + 9 * j + 3 * i] for i in range(3)]
            part = c[0] + c[1] * first[1] + c[2] * first[2]
            value = part if j == 0 else value + part * second[j]
        return value

    def moments(rows):
        s, t, u, v, w = (planes_ref[sub, at, rows, :] for at in range(5))
        fs, ft, fu, fv = powers(s), powers(t), powers(u), powers(v)
        gap = None
        for k in range(3):
            part = field(27 + k, fs, ft) * (field(54 + k, fu, fv) - field(k, fs, ft))
            gap = part if gap is None else gap + part
        base = [product(w, m, n) for n in ft[:3] for m in fs[:3]]
        return base + extra_products(w, fs, ft) + [x * gap for x in base]

    sums = accumulated(34, moments, UNROLL[2])
    for at, x in enumerate(sums):
        row = at if at < 25 else at + 7
        a_ref[row : row + 1, here] = total(x)


def lagrange_terms(i, j):
    axis = {0: [(1, -0.5), (2, 0.5)], 1: [(0, 1.0), (2, -1.0)], 2: [(1, 0.5), (2, 0.5)]}
    return [(m, n, p * q) for m, p in axis[i] for n, q in axis[j]]


def expanded(table, moments):
    high = moments.astype(BF16)
    rest = moments - high.astype(F32)
    middle = rest.astype(BF16)
    low = (rest - middle.astype(F32)).astype(BF16)
    return dot(table, high) + dot(table, middle) + dot(table, low)


def owner_kernel(in_ref, expand_ref, force_ref, mass_ref):
    chunks = in_ref.shape[0]
    segments = force_ref.shape[1]
    sums = jnp.zeros((2 * in_ref.shape[1], segments), F32)
    for at in range(0, chunks, 2):
        terms = jnp.concatenate([in_ref[at], in_ref[at + 1]], axis=1)
        hot = one_hot(terms[52:53, :].astype(jnp.int32), segments)
        sums = sums + dot_nt(stack2(terms), hot)
    sums = joined(sums)
    force_ref[...] = sums[0:27, :]
    moments = jnp.concatenate([sums[27:52, :], jnp.zeros((7, segments), F32)], axis=0)
    mass_ref[...] = expanded(expand_ref[...], moments)


def vmem(mib):
    return pltpu.CompilerParams(vmem_limit_bytes=mib << 20)


def from_patches(block):
    patches = lax.axis_size("patch")
    parts = [block]
    for d in range(1, patches):
        parts.append(lax.ppermute(block, "patch", [((i + d) % patches, i) for i in range(patches)]))
    return jnp.concatenate(parts, axis=0)


def from_chips(column):
    segs = lax.axis_size("seg")
    parts = [column]
    for d in range(1, segs // 2):
        parts.append(lax.ppermute(column, "seg", [(i ^ (2 * d), i) for i in range(segs)]))
    return jnp.concatenate(parts, axis=0)


def from_core(plane):
    return lax.ppermute(plane, "seg", [(i ^ 1, i) for i in range(lax.axis_size("seg"))])


def relative_owner(owner):
    patches, segs = lax.axis_size("patch"), lax.axis_size("seg")
    mine = lax.axis_index("seg")
    patch = jnp.mod(owner // segs - lax.axis_index("patch") + patches, patches)
    seg = jnp.bitwise_xor(owner % segs, mine)
    return (seg % 2) * (patches * segs // 2) + (seg // 2) * patches + patch


def shards(
    slave_local,
    owner_route,
    master_local,
    quad_slave,
    quad_master,
    quad_weight,
    slave_coords,
    slave_disp,
    slave_normals,
    multipliers,
    master_coords,
    master_disp,
):
    pairs = slave_local.shape[0]
    segments = slave_coords.shape[2]
    devices = lax.axis_size(AXES)
    cap = 2 * pairs // devices
    blocks = pairs // BLOCK
    steps = blocks // SUB
    wide = SUB * BLOCK

    slave_coords, slave_disp, slave_normals, multipliers, master_coords, master_disp = (
        pltpu.with_memory_space_constraint(jnp.transpose(x, (1, 0, 2)), pltpu.HBM)
        for x in (slave_coords, slave_disp, slave_normals, multipliers, master_coords, master_disp)
    )
    qs, qm, qw, sl, ml, owner = (
        pltpu.with_memory_space_constraint(x, pltpu.HBM)
        for x in (
            quad_slave.reshape(2 * pairs, 128),
            quad_master.reshape(2 * pairs, 128),
            quad_weight,
            slave_local.reshape(1, pairs),
            master_local.reshape(1, pairs),
            owner_route.reshape(1, pairs),
        )
    )
    block, rows = pl.pallas_call(
        table_kernel,
        out_shape=[jax.ShapeDtypeStruct((segments // 4, 128), F32), jax.ShapeDtypeStruct((1, pairs), jnp.int32)],
        scratch_shapes=[pltpu.VMEM((128, segments // 4), F32)],
        name="table",
    )(master_coords, master_disp, owner, ml)
    column = from_patches(block)

    planes_spec = pl.BlockSpec((SUB, 5, 128, BLOCK), lambda i: (i, 0, 0, 0))
    row_spec = pl.BlockSpec((1, wide), lambda i: (0, i))

    def whole(x):
        return pl.BlockSpec(x.shape, lambda i: (0,) * len(x.shape))

    def terms_call(first, last, previous):

        def at(spec, dim):
            return pl.BlockSpec(spec, lambda i: tuple(i + first if d == dim else 0 for d in range(2)))

        weight = at((wide, 128), 0)
        quad = at((2 * wide, 128), 0)
        row = at((1, wide), 1)
        return pl.pallas_call(
            terms_kernel,
            grid=(last - first,),
            in_specs=[quad, quad, weight, row, row, whole(multipliers)] + [pl.BlockSpec(memory_space=pl.ANY)] * len(previous),
            out_specs=[
                at((81, wide), 1), at((56, wide), 1), pl.BlockSpec((SUB, 5, 128, BLOCK), lambda i: (i + first, 0, 0, 0)),
            ],
            out_shape=[
                jax.ShapeDtypeStruct((81, pairs), F32),
                jax.ShapeDtypeStruct((56, pairs), F32),
                pltpu.HBM((blocks, 5, 128, BLOCK), F32),
            ],
            scratch_shapes=[
                pltpu.VMEM((SUB, 18, 128, BLOCK), F32),
                pltpu.VMEM((SUB, 9, 16, BLOCK), F32),
                pltpu.VMEM((64, segments), BF16),
            ],
            input_output_aliases={6 + i: i for i in range(len(previous))},
            compiler_params=vmem(16),
            cost_estimate=pl.CostEstimate(flops=10**9, transcendentals=0, bytes_accessed=15 * 10**6),
            name="terms",
        )(qs, qm, qw, sl, ml, multipliers, *previous)

    cut = 3 * steps // 8
    done = terms_call(0, cut, ())
    column, done = lax.optimization_barrier((column, done))
    plane = from_chips(column)
    done = terms_call(cut, steps, done)
    plane, (coupling, terms, quads) = lax.optimization_barrier((plane, done))
    other = from_core(plane)
    plane, other, quads = (pltpu.with_memory_space_constraint(x, pltpu.HBM) for x in (plane, other, quads))

    shape = (devices, 56, 128) if cap == 128 else (devices * cap // 256, 56, 256)
    outgoing = pl.pallas_call(
        functools.partial(slots_kernel, devices=devices, cap=cap),
        out_shape=jax.ShapeDtypeStruct(shape, F32),
        scratch_shapes=[pltpu.VMEM((112 * devices * cap // 256, pairs), BF16)],
        compiler_params=vmem(24),
        name="slots",
    )(owner, terms)
    if cap != 128:
        outgoing = outgoing.reshape(shape[0], 56, 256 // cap, cap).transpose(0, 2, 1, 3).reshape(devices, 56, cap)
    incoming = lax.all_to_all(outgoing, AXES, split_axis=0, concat_axis=0, tiled=True)
    if cap != 128:
        incoming = (
            incoming.reshape(devices * cap // 128, 128 // cap, 56, cap).transpose(0, 2, 1, 3).reshape(-1, 56, 128)
        )

    expand = jnp.asarray(expansion(powers=True), BF16)
    hbm = pl.BlockSpec(memory_space=pl.ANY)
    weighted_gap, slave_mass = pl.pallas_call(
        gap_kernel,
        grid=(steps,),
        in_specs=[
            pl.BlockSpec(memory_space=pltpu.SMEM), planes_spec, whole(sl), whole(ml),
            whole(slave_coords), whole(slave_disp), whole(slave_normals), whole(expand), hbm, hbm,
        ],
        out_specs=[pl.BlockSpec((9, segments), lambda i: (0, 0)), pl.BlockSpec((81, segments), lambda i: (0, 0))],
        out_shape=[jax.ShapeDtypeStruct((9, segments), F32), jax.ShapeDtypeStruct((81, segments), F32)],
        scratch_shapes=[
            pltpu.VMEM((devices * segments // 4, 128), F32),
            pltpu.VMEM((128, segments), BF16),
            pltpu.VMEM((48, segments), F32),
            pltpu.VMEM((48, pairs), F32),
            pltpu.VMEM((SUB, BLOCK, 128), F32),
            pltpu.VMEM((64, pairs), F32),
            pltpu.VMEM((SUB, 81, 8, BLOCK), F32),
            pltpu.VMEM((segments, pairs), BF16),
            pltpu.SemaphoreType.DMA((2,)),
        ],
        compiler_params=vmem(24),
        cost_estimate=pl.CostEstimate(flops=2 * 10**9, transcendentals=0, bytes_accessed=30 * 10**6),
        name="gap",
    )(rows, quads, sl, ml, slave_coords, slave_disp, slave_normals, expand, plane, other)

    expand = jnp.asarray(expansion(powers=False), BF16)
    force, master_mass = pl.pallas_call(
        owner_kernel,
        out_shape=[jax.ShapeDtypeStruct((27, segments), F32), jax.ShapeDtypeStruct((81, segments), F32)],
        compiler_params=vmem(16),
        name="owner",
    )(incoming, expand)
    return coupling, weighted_gap, slave_mass, force, master_mass


def solution(mesh):
    split = P(AXES)
    table = P(None, None, AXES)
    return jax.shard_map(
        shards,
        mesh=mesh,
        in_specs=(
            split, P(AXES, None), split, P(AXES, None, None), P(AXES, None, None), P(AXES, None),
            table, table, table, table, table, table,
        ),
        out_specs=(P(None, AXES),) * 5,
        check_vma=False,
    )
```

```python
import functools

import jax
import jax.numpy as jnp
import numpy as np
from jax import lax
from jax.experimental import pallas as pl
from jax.experimental.pallas import tpu as pltpu
from jax.sharding import PartitionSpec as P

AXES = ("patch", "seg")
BLOCK = 128
SUB = 2
GAP_FLOPS = 2 * 10**9
GAP_BYTES = 60 * 10**6
UNROLL = (16, 16, 16)
F32 = jnp.float32
BF16 = jnp.bfloat16


LAGRANGE = np.array([(0, -0.5, 0.5), (1, 0, -1), (0, 0.5, 0.5)], np.float32)


def from_powers():
    nodes = np.einsum("jn,im->jinm", LAGRANGE, LAGRANGE).reshape(9, 9)
    table = np.zeros((88, 96), np.float32)
    for at, column in enumerate(np.einsum("ac,bd->cdab", nodes, nodes).reshape(81, 81)):
        table[:81, 32 * (at // 27) + at % 27] = column
    return table


def power_products():
    return np.array([[np.convolve(p, q) for q in LAGRANGE] for p in LAGRANGE], np.float32)


def extra_moments():
    return [(m, n) for m in (3, 4) for n in range(5)] + [(m, n) for m in range(3) for n in (3, 4)]


def expansion():
    axis = power_products()
    table = np.zeros((81, 32), np.float32)
    columns = [(m, n) for n in range(3) for m in range(3)] + extra_moments()
    for b in range(9):
        for c in range(9):
            for at, (m, n) in enumerate(columns):
                table[9 * b + c, at] = axis[b % 3, c % 3, m] * axis[b // 3, c // 3, n]
    return table


def powers(t):
    square = t * t
    return [None, t, square, square * t, square * square]


def power_rows(x):
    def along(at, stride):
        out = [None] * 9
        for q in range(3):
            low, middle, high = (at[q * (4 - stride) + stride * i] for i in range(3))
            for i, block in enumerate((middle, 0.5 * (high - low), 0.5 * (high + low) - middle)):
                out[q * (4 - stride) + stride * i] = block
        return out

    return along(along(x, 1), 3)


def split2(x):
    high = x.astype(BF16)
    low = (x - high.astype(F32)).astype(BF16)
    return high, low


def stack2(x):
    high = x.astype(BF16).astype(F32)
    return jnp.concatenate([high, x - high], axis=0).astype(BF16)


def dot(a, b):
    return jnp.dot(a, b, preferred_element_type=F32)


def dot_nt(a, b):
    return lax.dot_general(a, b, (((1,), (1,)), ((), ())), preferred_element_type=F32)


def joined(product):
    half = product.shape[0] // 2
    return product[:half] + product[half:]


def one_hot(index_row, rows):
    at = lax.broadcasted_iota(jnp.int32, (rows, index_row.shape[1]), 0)
    return jnp.where(at == index_row, 1.0, 0.0).astype(BF16)


def total(x):
    return jnp.sum(x, axis=0, keepdims=True)


def merged(x, y, distance):
    rows = lax.broadcasted_iota(jnp.int32, (8, BLOCK), 0)
    first = (rows & distance) == 0
    if distance == 4:
        return jnp.where(first, x, y) + pltpu.roll(jnp.where(first, y, x), 4, 0)
    return jnp.where(first, x, y) + jnp.where(first, pltpu.roll(x, 8 - distance, 0), pltpu.roll(y, distance, 0))


def put_totals(ref, row, lanes, sums):
    for at in range(0, len(sums), 8):
        part = list(sums[at : at + 8])
        if len(part) == 1:
            ref[row + at : row + at + 1, lanes] = total(part[0])
            continue
        count = len(part)
        part = part + part[:1] * (8 - count)
        for distance in (4, 2, 1):
            part = [merged(part[k], part[k + distance], distance) for k in range(distance)]
        ref[row + at : row + at + count, lanes] = part[0][:count]


def planes(ref, sub):
    at = 2 * BLOCK * sub
    return ref[pl.ds(at, BLOCK, stride=2), :].T, ref[pl.ds(at + 1, BLOCK, stride=2), :].T


def product(*factors):
    value = None
    for x in factors:
        if x is not None:
            value = x if value is None else value * x
    return value


def extra_products(w, first, second):
    weighted = [product(w, x) for x in first]
    return [product(weighted[m], second[n]) for m, n in extra_moments()]


def accumulated(count, body, unroll):
    def step(c, sums):
        at = c * 8 if isinstance(c, int) else pl.multiple_of(c * 8, 8)
        return tuple(x + y for x, y in zip(sums, body(pl.ds(at, 8))))

    start = tuple(jnp.zeros((8, BLOCK), F32) for _ in range(count))
    return lax.fori_loop(0, 16, step, start, unroll=unroll)


def fill_rows(table_ref, start, blocks):
    half = table_ref.shape[0] // 2
    for a, block in enumerate(blocks):
        high, low = split2(block)
        at = start + 3 * a
        table_ref[at : at + 3, :] = high
        table_ref[at + half : at + half + 3, :] = low


def terms_kernel(qs_ref, qm_ref, w_ref, sl_ref, ml_ref, lam_ref, couple_ref, *rest):
    coupling_ref, terms_ref, planes_ref, shape_ref, c_ref, block_ref, lam_table_ref = rest[-7:]
    segments = lam_ref.shape[2]

    @pl.when(pl.program_id(0) == 0)
    def _():
        c_ref[...] = jnp.zeros_like(c_ref)
        fill_rows(lam_table_ref, 0, [lam_ref[a] for a in range(9)])

    for sub in range(SUB):
        w = w_ref[sub * BLOCK : (sub + 1) * BLOCK, :].T
        for at, plane in enumerate((*planes(qs_ref, sub), *planes(qm_ref, sub), w)):
            planes_ref[sub, at] = plane
    lam = joined(dot(lam_table_ref[...], one_hot(sl_ref[...], segments)))
    for sub in range(SUB):
        crossed_sums(sub, planes_ref, shape_ref, c_ref, terms_ref)
    moments = c_ref[...]
    coupling = expanded(couple_ref[...], moments)
    coupling_ref[...] = coupling[0:81]
    for a in range(9):
        block_ref[a, 0:9, :] = coupling[9 * a : 9 * a + 9]
    for k in range(3):
        force = block_ref[0, 0:9, :] * lam[k : k + 1, :]
        for a in range(1, 9):
            force = force + block_ref[a, 0:9, :] * lam[3 * a + k : 3 * a + k + 1, :]
        terms_ref[9 * k : 9 * k + 9, :] = force
    terms_ref[27:36, :] = moments[0:9]
    terms_ref[52:53, :] = ml_ref[...].astype(F32)
    terms_ref[53:56, :] = jnp.zeros((3, SUB * BLOCK), F32)


def crossed_sums(sub, planes_ref, shape_ref, c_ref, terms_ref):
    lanes = slice(sub * BLOCK, (sub + 1) * BLOCK)

    def prepared(rows):
        s, t, u, v, w = (planes_ref[sub, at, rows, :] for at in range(5))
        fs, ft, fu, fv = powers(s), powers(t), powers(u), powers(v)
        for j in range(3):
            for i in range(3):
                if i + j > 0:
                    shape_ref[sub, 3 * j + i, rows, :] = product(fu[i], fv[j])
                shape_ref[sub, 9 + 3 * j + i, rows, :] = product(w, fs[i], ft[j])
        return extra_products(w, fu, fv)

    put_totals(terms_ref, 36, lanes, accumulated(16, prepared, UNROLL[0]))
    for j in range(3):

        def crossed(rows):
            master = [None] + [shape_ref[sub, b, rows, :] for b in range(1, 9)]
            slave = [shape_ref[sub, 9 + 3 * j + i, rows, :] for i in range(3)]
            return [product(x, y) for x in slave for y in master]

        put_totals(c_ref, 32 * j, lanes, accumulated(27, crossed, UNROLL[1]))


def slots_kernel(owner_ref, terms_ref, out_ref, left_ref, *, devices, cap):
    pairs = owner_ref.shape[1]
    width = 256
    per = width // cap
    groups = devices // per
    owner = owner_ref[...]
    upper = jnp.where(
        lax.broadcasted_iota(jnp.int32, (width, width), 0) < lax.broadcasted_iota(jnp.int32, (width, width), 1),
        1.0,
        0.0,
    ).astype(BF16)
    carry = jnp.zeros((devices, 1), F32)
    ranks = []
    for at in range(0, pairs, width):
        mine = one_hot(owner[:, at : at + width], devices)
        before = dot(mine, upper) + carry
        wide = mine.astype(F32)
        ranks.append(total(wide * before))
        carry = carry + jnp.sum(wide, axis=1, keepdims=True)
    rank = jnp.concatenate(ranks, axis=1).astype(jnp.int32)
    group = owner // per
    column = (owner - group * per) * cap + rank
    place = one_hot(column, width)
    both = stack2(terms_ref[...])
    rows = both.shape[0]
    for g in range(groups):
        left_ref[g * rows : (g + 1) * rows, :] = both * jnp.where(group == g, 1.0, 0.0).astype(BF16)
    sent = dot_nt(left_ref[...], place)
    for g in range(groups):
        block = joined(sent[g * rows : (g + 1) * rows])
        if cap == 128:
            out_ref[2 * g] = block[:, :128]
            out_ref[2 * g + 1] = block[:, 128:]
        else:
            out_ref[g] = block


def table_kernel(coords_ref, disp_ref, owner_ref, local_ref, out_ref, place_ref, rows_ref):
    place_ref[...] = relative_owner(owner_ref[...]) * out_ref.shape[0] + local_ref[...] % 128
    rows_ref[...] = jnp.zeros_like(rows_ref)
    for i, block in enumerate(power_rows([coords_ref[a] + disp_ref[a] for a in range(9)])):
        for c in range(block.shape[1] // 128):
            at = 32 * c + 3 * i
            rows_ref[at : at + 3, :] = block[:, 128 * c : 128 * (c + 1)]
    out_ref[...] = rows_ref[...].T


def gap_kernel(
    row_ref, planes_ref, sl_ref, ml_ref, coords_ref, disp_ref, normals_ref, expand_ref, near_ref, far_ref,
    gap_ref, mass_ref, table_ref, slave_ref, sums_ref, a_ref, picked_ref, coef_ref, wide_ref, hot_ref, sems,
):
    segments = coords_ref.shape[2]
    step = pl.program_id(0)

    @pl.when(step == 0)
    def _():
        half = near_ref.shape[0]
        copies = [
            pltpu.make_async_copy(near_ref, table_ref.at[pl.ds(0, half)], sems.at[0]),
            pltpu.make_async_copy(far_ref, table_ref.at[pl.ds(half, half)], sems.at[1]),
        ]
        for copy in copies:
            copy.start()
        a_ref[...] = jnp.zeros_like(a_ref)
        slave_ref[...] = jnp.zeros_like(slave_ref)
        fill_rows(slave_ref, 0, power_rows([coords_ref[a] + disp_ref[a] for a in range(9)]))
        fill_rows(slave_ref, 32, power_rows([normals_ref[a] for a in range(9)]))
        hot_ref[...] = one_hot(sl_ref[...], segments)
        coef_ref[0:64, :] = joined(dot(slave_ref[...], hot_ref[...]))
        for copy in copies:
            copy.wait()

    for sub in range(SUB):
        gap_block(sub, step, row_ref, ml_ref, planes_ref, table_ref, picked_ref, coef_ref, wide_ref, a_ref, segments)

    @pl.when(step == pl.num_programs(0) - 1)
    def _():
        sums_ref[...] = joined(dot_nt(stack2(a_ref[...]), hot_ref[...]))
        for j in range(3):
            for i in range(3):
                row = None
                for m, n, sign in lagrange_terms(i, j):
                    part = sums_ref[32 + 3 * n + m : 33 + 3 * n + m, :] * sign
                    row = part if row is None else row + part
                gap_ref[3 * j + i : 3 * j + i + 1, :] = row
        mass_ref[...] = expanded(expand_ref[...], sums_ref[0:32, :])


def gap_block(sub, step, row_ref, ml_ref, planes_ref, table_ref, picked_ref, coef_ref, wide_ref, a_ref, segments):
    start = pl.multiple_of((step * SUB + sub) * BLOCK, BLOCK)
    for p in range(BLOCK):
        picked_ref[sub, p : p + 1, :] = table_ref[pl.ds(row_ref[0, start + p], 1), :]
    picked = picked_ref[sub].T
    quarter = ml_ref[:, pl.ds(start, BLOCK)] // 128
    position = picked[0:32]
    for c in range(1, segments // 128):
        position = jnp.where(quarter == c, picked[32 * c : 32 * c + 32], position)
    here = pl.ds(start, BLOCK)
    for row in range(54):
        at = row if row < 27 else row + 5
        wide_ref[sub, row] = jnp.broadcast_to(coef_ref[at : at + 1, here], (8, BLOCK))
    for row in range(27):
        wide_ref[sub, 54 + row] = jnp.broadcast_to(position[row : row + 1], (8, BLOCK))

    def field(row, first, second):
        value = None
        for j in range(3):
            c = [wide_ref[sub, row + 9 * j + 3 * i] for i in range(3)]
            part = c[0] + c[1] * first[1] + c[2] * first[2]
            value = part if j == 0 else value + part * second[j]
        return value

    def moments(rows):
        s, t, u, v, w = (planes_ref[sub, at, rows, :] for at in range(5))
        fs, ft, fu, fv = powers(s), powers(t), powers(u), powers(v)
        gap = None
        for k in range(3):
            part = field(27 + k, fs, ft) * (field(54 + k, fu, fv) - field(k, fs, ft))
            gap = part if gap is None else gap + part
        base = [product(w, m, n) for n in ft[:3] for m in fs[:3]]
        return base + extra_products(w, fs, ft) + [x * gap for x in base]

    sums = accumulated(34, moments, UNROLL[2])
    put_totals(a_ref, 0, here, sums[:25])
    put_totals(a_ref, 32, here, sums[25:])


def lagrange_terms(i, j):
    axis = {0: [(1, -0.5), (2, 0.5)], 1: [(0, 1.0), (2, -1.0)], 2: [(1, 0.5), (2, 0.5)]}
    return [(m, n, p * q) for m, p in axis[i] for n, q in axis[j]]


def expanded(table, moments):
    high = moments.astype(BF16)
    rest = moments - high.astype(F32)
    middle = rest.astype(BF16)
    low = (rest - middle.astype(F32)).astype(BF16)
    return dot(table, high) + dot(table, middle) + dot(table, low)


def owner_kernel(in_ref, expand_ref, force_ref, mass_ref):
    chunks = in_ref.shape[0]
    segments = force_ref.shape[1]
    rows = 2 * in_ref.shape[1]
    half = segments // 2
    sums = jnp.zeros((2 * rows, half), F32)
    for at in range(0, chunks, 2):
        terms = jnp.concatenate([in_ref[at], in_ref[at + 1]], axis=1)
        local = terms[52:53, :].astype(jnp.int32)
        both = stack2(terms)
        upper = jnp.where(local >= half, 1.0, 0.0).astype(BF16)
        left = jnp.concatenate([both * (1 - upper), both * upper], axis=0)
        sums = sums + dot_nt(left, one_hot(local % half, half))
    sums = jnp.concatenate([sums[:rows], sums[rows:]], axis=1)
    sums = joined(sums)
    force_ref[...] = sums[0:27, :]
    moments = jnp.concatenate([sums[27:52, :], jnp.zeros((7, segments), F32)], axis=0)
    mass_ref[...] = expanded(expand_ref[...], moments)


def vmem(mib):
    return pltpu.CompilerParams(vmem_limit_bytes=mib << 20)


def from_patches(block):
    patches = lax.axis_size("patch")
    parts = [block]
    for d in range(1, patches):
        parts.append(lax.ppermute(block, "patch", [((i + d) % patches, i) for i in range(patches)]))
    return jnp.concatenate(parts, axis=0)


def from_chips(column):
    segs = lax.axis_size("seg")
    parts = [column]
    for d in range(1, segs // 2):
        parts.append(lax.ppermute(column, "seg", [(i ^ (2 * d), i) for i in range(segs)]))
    return jnp.concatenate(lax.optimization_barrier(parts), axis=0)


def from_core(plane):
    return lax.ppermute(plane, "seg", [(i ^ 1, i) for i in range(lax.axis_size("seg"))])


def relative_owner(owner):
    patches, segs = lax.axis_size("patch"), lax.axis_size("seg")
    mine = lax.axis_index("seg")
    patch = jnp.mod(owner // segs - lax.axis_index("patch") + patches, patches)
    seg = jnp.bitwise_xor(owner % segs, mine)
    return (seg % 2) * (patches * segs // 2) + (seg // 2) * patches + patch


def shards(
    slave_local,
    owner_route,
    master_local,
    quad_slave,
    quad_master,
    quad_weight,
    slave_coords,
    slave_disp,
    slave_normals,
    multipliers,
    master_coords,
    master_disp,
):
    pairs = slave_local.shape[0]
    segments = slave_coords.shape[2]
    devices = lax.axis_size(AXES)
    cap = 2 * pairs // devices
    blocks = pairs // BLOCK
    steps = blocks // SUB
    wide = SUB * BLOCK

    slave_coords, slave_disp, slave_normals, multipliers, master_coords, master_disp = (
        pltpu.with_memory_space_constraint(jnp.transpose(x, (1, 0, 2)), pltpu.HBM)
        for x in (slave_coords, slave_disp, slave_normals, multipliers, master_coords, master_disp)
    )
    qs, qm, qw, sl, ml, owner = (
        pltpu.with_memory_space_constraint(x, pltpu.HBM)
        for x in (
            quad_slave.reshape(2 * pairs, 128),
            quad_master.reshape(2 * pairs, 128),
            quad_weight,
            slave_local.reshape(1, pairs),
            master_local.reshape(1, pairs),
            owner_route.reshape(1, pairs),
        )
    )
    block, rows = pl.pallas_call(
        table_kernel,
        out_shape=[jax.ShapeDtypeStruct((segments // 4, 128), F32), jax.ShapeDtypeStruct((1, pairs), jnp.int32)],
        scratch_shapes=[pltpu.VMEM((128, segments // 4), F32)],
        name="table",
    )(master_coords, master_disp, owner, ml)
    column = from_patches(block)

    planes_spec = pl.BlockSpec((SUB, 5, 128, BLOCK), lambda i: (i, 0, 0, 0))
    row_spec = pl.BlockSpec((1, wide), lambda i: (0, i))

    def whole(x):
        return pl.BlockSpec(x.shape, lambda i: (0,) * len(x.shape))

    couple = pltpu.with_memory_space_constraint(jnp.asarray(from_powers(), BF16), pltpu.HBM)

    def terms_call(first, last, previous):

        def at(spec, dim):
            return pl.BlockSpec(spec, lambda i: tuple(i + first if d == dim else 0 for d in range(2)))

        weight = at((wide, 128), 0)
        quad = at((2 * wide, 128), 0)
        row = at((1, wide), 1)
        return pl.pallas_call(
            terms_kernel,
            grid=(last - first,),
            in_specs=[quad, quad, weight, row, row, whole(multipliers), whole(couple)] + [pl.BlockSpec(memory_space=pl.ANY)] * len(previous),
            out_specs=[
                at((81, wide), 1), at((56, wide), 1), pl.BlockSpec((SUB, 5, 128, BLOCK), lambda i: (i + first, 0, 0, 0)),
            ],
            out_shape=[
                jax.ShapeDtypeStruct((81, pairs), F32),
                jax.ShapeDtypeStruct((56, pairs), F32),
                pltpu.HBM((blocks, 5, 128, BLOCK), F32),
            ],
            scratch_shapes=[
                pltpu.VMEM((SUB, 18, 128, BLOCK), F32),
                pltpu.VMEM((96, wide), F32),
                pltpu.VMEM((9, 16, wide), F32),
                pltpu.VMEM((64, segments), BF16),
            ],
            input_output_aliases={7 + i: i for i in range(len(previous))},
            compiler_params=vmem(16),
            cost_estimate=pl.CostEstimate(flops=10**9, transcendentals=0, bytes_accessed=15 * 10**6),
            name="terms",
        )(qs, qm, qw, sl, ml, multipliers, couple, *previous)

    done = terms_call(0, steps, ())
    column, (coupling, terms, quads) = lax.optimization_barrier((column, done))
    plane = from_chips(column)
    other = from_core(plane)
    quads = pltpu.with_memory_space_constraint(quads, pltpu.HBM)

    shape = (devices, 56, 128) if cap == 128 else (devices * cap // 256, 56, 256)
    outgoing = pl.pallas_call(
        functools.partial(slots_kernel, devices=devices, cap=cap),
        out_shape=jax.ShapeDtypeStruct(shape, F32),
        scratch_shapes=[pltpu.VMEM((112 * devices * cap // 256, pairs), BF16)],
        compiler_params=vmem(24),
        name="slots",
    )(owner, terms)
    if cap != 128:
        outgoing = outgoing.reshape(shape[0], 56, 256 // cap, cap).transpose(0, 2, 1, 3).reshape(devices, 56, cap)
    incoming = lax.all_to_all(outgoing, AXES, split_axis=0, concat_axis=0, tiled=True)
    if cap != 128:
        incoming = (
            incoming.reshape(devices * cap // 128, 128 // cap, 56, cap).transpose(0, 2, 1, 3).reshape(-1, 56, 128)
        )

    expand = jnp.asarray(expansion(), BF16)
    hbm = pl.BlockSpec(memory_space=pl.ANY)
    weighted_gap, slave_mass = pl.pallas_call(
        gap_kernel,
        grid=(steps,),
        in_specs=[
            pl.BlockSpec(memory_space=pltpu.SMEM), planes_spec, whole(sl), whole(ml),
            whole(slave_coords), whole(slave_disp), whole(slave_normals), whole(expand), hbm, hbm,
        ],
        out_specs=[pl.BlockSpec((9, segments), lambda i: (0, 0)), pl.BlockSpec((81, segments), lambda i: (0, 0))],
        out_shape=[jax.ShapeDtypeStruct((9, segments), F32), jax.ShapeDtypeStruct((81, segments), F32)],
        scratch_shapes=[
            pltpu.VMEM((devices * segments // 4, 128), F32),
            pltpu.VMEM((128, segments), BF16),
            pltpu.VMEM((48, segments), F32),
            pltpu.VMEM((48, pairs), F32),
            pltpu.VMEM((SUB, BLOCK, 128), F32),
            pltpu.VMEM((64, pairs), F32),
            pltpu.VMEM((SUB, 81, 8, BLOCK), F32),
            pltpu.VMEM((segments, pairs), BF16),
            pltpu.SemaphoreType.DMA((2,)),
        ],
        compiler_params=vmem(24),
        cost_estimate=pl.CostEstimate(flops=GAP_FLOPS, transcendentals=0, bytes_accessed=GAP_BYTES),
        name="gap",
    )(rows, quads, sl, ml, slave_coords, slave_disp, slave_normals, expand, plane, other)

    force, master_mass = pl.pallas_call(
        owner_kernel,
        out_shape=[jax.ShapeDtypeStruct((27, segments), F32), jax.ShapeDtypeStruct((81, segments), F32)],
        compiler_params=vmem(16),
        name="owner",
    )(incoming, expand)
    return coupling, weighted_gap, slave_mass, force, master_mass


def solution(mesh):
    split = P(AXES)
    table = P(None, None, AXES)
    return jax.shard_map(
        shards,
        mesh=mesh,
        in_specs=(
            split, P(AXES, None), split, P(AXES, None, None), P(AXES, None, None), P(AXES, None),
            table, table, table, table, table, table,
        ),
        out_specs=(P(None, AXES),) * 5,
        check_vma=False,
    )
```

```python
import functools

import jax
import jax.numpy as jnp
import numpy as np
from jax import lax
from jax.experimental import pallas as pl
from jax.experimental.pallas import tpu as pltpu
from jax.sharding import PartitionSpec as P

AXES = ("patch", "seg")
BLOCK = 128
SUB = 4
GAP_FLOPS = 2 * 10**9
GAP_BYTES = 60 * 10**6
UNROLL = (16, 16, 16)
F32 = jnp.float32
BF16 = jnp.bfloat16


LAGRANGE = np.array([(0, -0.5, 0.5), (1, 0, -1), (0, 0.5, 0.5)], np.float32)


def from_powers():
    nodes = np.einsum("jn,im->jinm", LAGRANGE, LAGRANGE).reshape(9, 9)
    table = np.zeros((88, 96), np.float32)
    for at, column in enumerate(np.einsum("ac,bd->cdab", nodes, nodes).reshape(81, 81)):
        table[:81, 32 * (at // 27) + at % 27] = column
    return np.concatenate([table, table], axis=1)


def power_products():
    return np.array([[np.convolve(p, q) for q in LAGRANGE] for p in LAGRANGE], np.float32)


def extra_moments():
    return [(m, n) for m in (3, 4) for n in range(5)] + [(m, n) for m in range(3) for n in (3, 4)]


def expansion():
    axis = power_products()
    table = np.zeros((81, 32), np.float32)
    columns = [(m, n) for n in range(3) for m in range(3)] + extra_moments()
    for b in range(9):
        for c in range(9):
            for at, (m, n) in enumerate(columns):
                table[9 * b + c, at] = axis[b % 3, c % 3, m] * axis[b // 3, c // 3, n]
    return table


def powers(t):
    square = t * t
    return [None, t, square, square * t, square * square]


def power_rows(x):
    def along(at, stride):
        out = [None] * 9
        for q in range(3):
            low, middle, high = (at[q * (4 - stride) + stride * i] for i in range(3))
            for i, block in enumerate((middle, 0.5 * (high - low), 0.5 * (high + low) - middle)):
                out[q * (4 - stride) + stride * i] = block
        return out

    return along(along(x, 1), 3)


def split2(x):
    high = x.astype(BF16)
    low = (x - high.astype(F32)).astype(BF16)
    return high, low


def stack2(x):
    high = x.astype(BF16).astype(F32)
    return jnp.concatenate([high, x - high], axis=0).astype(BF16)


def dot(a, b):
    return jnp.dot(a, b, preferred_element_type=F32)


def dot_nt(a, b):
    return lax.dot_general(a, b, (((1,), (1,)), ((), ())), preferred_element_type=F32)


def joined(product):
    half = product.shape[0] // 2
    return product[:half] + product[half:]


def one_hot(index_row, rows):
    at = lax.broadcasted_iota(jnp.int32, (rows, index_row.shape[1]), 0)
    return jnp.where(at == index_row, 1.0, 0.0).astype(BF16)


def total(x):
    return jnp.sum(x, axis=0, keepdims=True)


def merged(x, y, distance):
    rows = lax.broadcasted_iota(jnp.int32, (8, BLOCK), 0)
    first = (rows & distance) == 0
    if distance == 4:
        return jnp.where(first, x, y) + pltpu.roll(jnp.where(first, y, x), 4, 0)
    return jnp.where(first, x, y) + jnp.where(first, pltpu.roll(x, 8 - distance, 0), pltpu.roll(y, distance, 0))


def put_totals(ref, row, lanes, sums):
    for at in range(0, len(sums), 8):
        part = list(sums[at : at + 8])
        if len(part) == 1:
            ref[row + at : row + at + 1, lanes] = total(part[0])
            continue
        count = len(part)
        part = part + part[:1] * (8 - count)
        for distance in (4, 2, 1):
            part = [merged(part[k], part[k + distance], distance) for k in range(distance)]
        ref[row + at : row + at + count, lanes] = part[0][:count]


def planes(ref, sub):
    at = 2 * BLOCK * sub
    return ref[pl.ds(at, BLOCK, stride=2), :].T, ref[pl.ds(at + 1, BLOCK, stride=2), :].T


def product(*factors):
    value = None
    for x in factors:
        if x is not None:
            value = x if value is None else value * x
    return value


def extra_products(w, first, second):
    weighted = [product(w, x) for x in first]
    return [product(weighted[m], second[n]) for m, n in extra_moments()]


def accumulated(count, body, unroll):
    def step(c, sums):
        at = c * 8 if isinstance(c, int) else pl.multiple_of(c * 8, 8)
        return tuple(x + y for x, y in zip(sums, body(pl.ds(at, 8))))

    start = tuple(jnp.zeros((8, BLOCK), F32) for _ in range(count))
    return lax.fori_loop(0, 16, step, start, unroll=unroll)


def fill_rows(table_ref, start, blocks):
    half = table_ref.shape[0] // 2
    for a, block in enumerate(blocks):
        high, low = split2(block)
        at = start + 3 * a
        table_ref[at : at + 3, :] = high
        table_ref[at + half : at + half + 3, :] = low


def terms_kernel(qs_ref, qm_ref, w_ref, sl_ref, ml_ref, lam_ref, couple_ref, *rest):
    coupling_ref, terms_ref, planes_ref, shape_ref, c_ref, block_ref, lam_table_ref = rest[-7:]
    segments = lam_ref.shape[2]

    @pl.when(pl.program_id(0) == 0)
    def _():
        c_ref[...] = jnp.zeros_like(c_ref)
        fill_rows(lam_table_ref, 0, [lam_ref[a] for a in range(9)])

    for sub in range(SUB):
        w = w_ref[sub * BLOCK : (sub + 1) * BLOCK, :].T
        for at, plane in enumerate((*planes(qs_ref, sub), *planes(qm_ref, sub), w)):
            planes_ref[sub, at] = plane
    lam = joined(dot(lam_table_ref[...], one_hot(sl_ref[...], segments)))
    for sub in range(SUB):
        crossed_sums(sub, planes_ref, shape_ref, c_ref, terms_ref)
    moments = c_ref[...]
    coupling = dot(couple_ref[...], stack2(moments))
    coupling_ref[...] = coupling[0:81]
    for a in range(9):
        block_ref[a, 0:9, :] = coupling[9 * a : 9 * a + 9]
    for k in range(3):
        force = block_ref[0, 0:9, :] * lam[k : k + 1, :]
        for a in range(1, 9):
            force = force + block_ref[a, 0:9, :] * lam[3 * a + k : 3 * a + k + 1, :]
        terms_ref[9 * k : 9 * k + 9, :] = force
    terms_ref[27:36, :] = moments[0:9]
    terms_ref[52:53, :] = ml_ref[...].astype(F32)
    terms_ref[53:56, :] = jnp.zeros((3, SUB * BLOCK), F32)


def crossed_sums(sub, planes_ref, shape_ref, c_ref, terms_ref):
    lanes = slice(sub * BLOCK, (sub + 1) * BLOCK)

    def prepared(rows):
        s, t, u, v, w = (planes_ref[sub, at, rows, :] for at in range(5))
        fs, ft, fu, fv = powers(s), powers(t), powers(u), powers(v)
        for j in range(3):
            for i in range(3):
                if i + j > 0:
                    shape_ref[sub, 3 * j + i, rows, :] = product(fu[i], fv[j])
                shape_ref[sub, 9 + 3 * j + i, rows, :] = product(w, fs[i], ft[j])
        return extra_products(w, fu, fv)

    put_totals(terms_ref, 36, lanes, accumulated(16, prepared, UNROLL[0]))
    for j in range(3):

        def crossed(rows):
            master = [None] + [shape_ref[sub, b, rows, :] for b in range(1, 9)]
            slave = [shape_ref[sub, 9 + 3 * j + i, rows, :] for i in range(3)]
            return [product(x, y) for x in slave for y in master]

        put_totals(c_ref, 32 * j, lanes, accumulated(27, crossed, UNROLL[1]))


def slots_kernel(owner_ref, terms_ref, out_ref, left_ref, *, devices, cap):
    pairs = owner_ref.shape[1]
    width = 256
    per = width // cap
    groups = devices // per
    owner = owner_ref[...]
    upper = jnp.where(
        lax.broadcasted_iota(jnp.int32, (width, width), 0) < lax.broadcasted_iota(jnp.int32, (width, width), 1),
        1.0,
        0.0,
    ).astype(BF16)
    carry = jnp.zeros((devices, 1), F32)
    ranks = []
    for at in range(0, pairs, width):
        mine = one_hot(owner[:, at : at + width], devices)
        before = dot(mine, upper) + carry
        wide = mine.astype(F32)
        ranks.append(total(wide * before))
        carry = carry + jnp.sum(wide, axis=1, keepdims=True)
    rank = jnp.concatenate(ranks, axis=1).astype(jnp.int32)
    group = owner // per
    column = (owner - group * per) * cap + rank
    place = one_hot(column, width)
    both = stack2(terms_ref[...])
    rows = both.shape[0]
    for g in range(groups):
        left_ref[g * rows : (g + 1) * rows, :] = both * jnp.where(group == g, 1.0, 0.0).astype(BF16)
    sent = dot_nt(left_ref[...], place)
    for g in range(groups):
        block = joined(sent[g * rows : (g + 1) * rows])
        if cap == 128:
            out_ref[2 * g] = block[:, :128]
            out_ref[2 * g + 1] = block[:, 128:]
        else:
            out_ref[g] = block


def table_kernel(coords_ref, disp_ref, owner_ref, local_ref, out_ref, place_ref, rows_ref):
    place_ref[...] = relative_owner(owner_ref[...]) * out_ref.shape[0] + local_ref[...] % 128
    rows_ref[...] = jnp.zeros_like(rows_ref)
    for i, block in enumerate(power_rows([coords_ref[a] + disp_ref[a] for a in range(9)])):
        for c in range(block.shape[1] // 128):
            at = 32 * c + 3 * i
            rows_ref[at : at + 3, :] = block[:, 128 * c : 128 * (c + 1)]
    out_ref[...] = rows_ref[...].T


def gap_kernel(
    row_ref, planes_ref, sl_ref, ml_ref, coords_ref, disp_ref, normals_ref, expand_ref, near_ref, far_ref,
    gap_ref, mass_ref, table_ref, slave_ref, sums_ref, a_ref, picked_ref, coef_ref, wide_ref, hot_ref, sems,
):
    segments = coords_ref.shape[2]
    step = pl.program_id(0)

    @pl.when(step == 0)
    def _():
        half = near_ref.shape[0]
        copies = [
            pltpu.make_async_copy(near_ref, table_ref.at[pl.ds(0, half)], sems.at[0]),
            pltpu.make_async_copy(far_ref, table_ref.at[pl.ds(half, half)], sems.at[1]),
        ]
        for copy in copies:
            copy.start()
        a_ref[...] = jnp.zeros_like(a_ref)
        slave_ref[...] = jnp.zeros_like(slave_ref)
        fill_rows(slave_ref, 0, power_rows([coords_ref[a] + disp_ref[a] for a in range(9)]))
        fill_rows(slave_ref, 32, power_rows([normals_ref[a] for a in range(9)]))
        hot_ref[...] = one_hot(sl_ref[...], segments)
        coef_ref[0:64, :] = joined(dot(slave_ref[...], hot_ref[...]))
        for copy in copies:
            copy.wait()

    for sub in range(SUB):
        gap_block(sub, step, row_ref, ml_ref, planes_ref, table_ref, picked_ref, coef_ref, wide_ref, a_ref, segments)

    @pl.when(step == pl.num_programs(0) - 1)
    def _():
        sums_ref[...] = joined(dot_nt(stack2(a_ref[...]), hot_ref[...]))
        for j in range(3):
            for i in range(3):
                row = None
                for m, n, sign in lagrange_terms(i, j):
                    part = sums_ref[32 + 3 * n + m : 33 + 3 * n + m, :] * sign
                    row = part if row is None else row + part
                gap_ref[3 * j + i : 3 * j + i + 1, :] = row
        mass_ref[...] = expanded(expand_ref[...], sums_ref[0:32, :])


def gap_block(sub, step, row_ref, ml_ref, planes_ref, table_ref, picked_ref, coef_ref, wide_ref, a_ref, segments):
    start = pl.multiple_of((step * SUB + sub) * BLOCK, BLOCK)
    for p in range(BLOCK):
        picked_ref[sub, p : p + 1, :] = table_ref[pl.ds(row_ref[0, start + p], 1), :]
    picked = picked_ref[sub].T
    quarter = ml_ref[:, pl.ds(start, BLOCK)] // 128
    position = picked[0:32]
    for c in range(1, segments // 128):
        position = jnp.where(quarter == c, picked[32 * c : 32 * c + 32], position)
    here = pl.ds(start, BLOCK)
    for row in range(54):
        at = row if row < 27 else row + 5
        wide_ref[sub, row] = jnp.broadcast_to(coef_ref[at : at + 1, here], (8, BLOCK))
    for row in range(27):
        wide_ref[sub, 54 + row] = jnp.broadcast_to(position[row : row + 1], (8, BLOCK))

    def field(row, first, second):
        value = None
        for j in range(3):
            c = [wide_ref[sub, row + 9 * j + 3 * i] for i in range(3)]
            part = c[0] + c[1] * first[1] + c[2] * first[2]
            value = part if j == 0 else value + part * second[j]
        return value

    def moments(rows):
        s, t, u, v, w = (planes_ref[sub, at, rows, :] for at in range(5))
        fs, ft, fu, fv = powers(s), powers(t), powers(u), powers(v)
        gap = None
        for k in range(3):
            part = field(27 + k, fs, ft) * (field(54 + k, fu, fv) - field(k, fs, ft))
            gap = part if gap is None else gap + part
        base = [product(w, m, n) for n in ft[:3] for m in fs[:3]]
        return base + extra_products(w, fs, ft) + [x * gap for x in base]

    sums = accumulated(34, moments, UNROLL[2])
    put_totals(a_ref, 0, here, sums[:25])
    put_totals(a_ref, 32, here, sums[25:])


def lagrange_terms(i, j):
    axis = {0: [(1, -0.5), (2, 0.5)], 1: [(0, 1.0), (2, -1.0)], 2: [(1, 0.5), (2, 0.5)]}
    return [(m, n, p * q) for m, p in axis[i] for n, q in axis[j]]


def expanded(table, moments):
    high = moments.astype(BF16)
    rest = moments - high.astype(F32)
    middle = rest.astype(BF16)
    low = (rest - middle.astype(F32)).astype(BF16)
    return dot(table, high) + dot(table, middle) + dot(table, low)


def owner_kernel(in_ref, expand_ref, force_ref, mass_ref):
    chunks = in_ref.shape[0]
    segments = force_ref.shape[1]
    rows = 2 * in_ref.shape[1]
    half = segments // 2
    sums = jnp.zeros((2 * rows, half), F32)
    for at in range(0, chunks, 2):
        terms = jnp.concatenate([in_ref[at], in_ref[at + 1]], axis=1)
        local = terms[52:53, :].astype(jnp.int32)
        both = stack2(terms)
        upper = jnp.where(local >= half, 1.0, 0.0).astype(BF16)
        left = jnp.concatenate([both * (1 - upper), both * upper], axis=0)
        sums = sums + dot_nt(left, one_hot(local % half, half))
    sums = jnp.concatenate([sums[:rows], sums[rows:]], axis=1)
    sums = joined(sums)
    force_ref[...] = sums[0:27, :]
    moments = jnp.concatenate([sums[27:52, :], jnp.zeros((7, segments), F32)], axis=0)
    mass_ref[...] = expanded(expand_ref[...], moments)


def vmem(mib):
    return pltpu.CompilerParams(vmem_limit_bytes=mib << 20)


def from_patches(block):
    patches = lax.axis_size("patch")
    parts = [block]
    for d in range(1, patches):
        parts.append(lax.ppermute(block, "patch", [((i + d) % patches, i) for i in range(patches)]))
    return jnp.concatenate(parts, axis=0)


def from_chips(column):
    segs = lax.axis_size("seg")
    parts = [column]
    for d in range(1, segs // 2):
        parts.append(lax.ppermute(column, "seg", [(i ^ (2 * d), i) for i in range(segs)]))
    return jnp.concatenate(lax.optimization_barrier(parts), axis=0)


def from_core(plane):
    return lax.ppermute(plane, "seg", [(i ^ 1, i) for i in range(lax.axis_size("seg"))])


def relative_owner(owner):
    patches, segs = lax.axis_size("patch"), lax.axis_size("seg")
    mine = lax.axis_index("seg")
    patch = jnp.mod(owner // segs - lax.axis_index("patch") + patches, patches)
    seg = jnp.bitwise_xor(owner % segs, mine)
    return (seg % 2) * (patches * segs // 2) + (seg // 2) * patches + patch


def shards(
    slave_local,
    owner_route,
    master_local,
    quad_slave,
    quad_master,
    quad_weight,
    slave_coords,
    slave_disp,
    slave_normals,
    multipliers,
    master_coords,
    master_disp,
):
    pairs = slave_local.shape[0]
    segments = slave_coords.shape[2]
    devices = lax.axis_size(AXES)
    cap = 2 * pairs // devices
    blocks = pairs // BLOCK
    steps = blocks // SUB
    wide = SUB * BLOCK

    slave_coords, slave_disp, slave_normals, multipliers, master_coords, master_disp = (
        pltpu.with_memory_space_constraint(jnp.transpose(x, (1, 0, 2)), pltpu.HBM)
        for x in (slave_coords, slave_disp, slave_normals, multipliers, master_coords, master_disp)
    )
    qs, qm, qw, sl, ml, owner = (
        pltpu.with_memory_space_constraint(x, pltpu.HBM)
        for x in (
            quad_slave.reshape(2 * pairs, 128),
            quad_master.reshape(2 * pairs, 128),
            quad_weight,
            slave_local.reshape(1, pairs),
            master_local.reshape(1, pairs),
            owner_route.reshape(1, pairs),
        )
    )
    block, rows = pl.pallas_call(
        table_kernel,
        out_shape=[jax.ShapeDtypeStruct((segments // 4, 128), F32), jax.ShapeDtypeStruct((1, pairs), jnp.int32)],
        scratch_shapes=[pltpu.VMEM((128, segments // 4), F32)],
        name="table",
    )(master_coords, master_disp, owner, ml)
    column = from_patches(block)

    planes_spec = pl.BlockSpec((SUB, 5, 128, BLOCK), lambda i: (i, 0, 0, 0))
    row_spec = pl.BlockSpec((1, wide), lambda i: (0, i))

    def whole(x):
        return pl.BlockSpec(x.shape, lambda i: (0,) * len(x.shape))

    couple = pltpu.with_memory_space_constraint(jnp.asarray(from_powers(), BF16), pltpu.HBM)

    def terms_call(first, last, previous):

        def at(spec, dim):
            return pl.BlockSpec(spec, lambda i: tuple(i + first if d == dim else 0 for d in range(2)))

        weight = at((wide, 128), 0)
        quad = at((2 * wide, 128), 0)
        row = at((1, wide), 1)
        return pl.pallas_call(
            terms_kernel,
            grid=(last - first,),
            in_specs=[quad, quad, weight, row, row, whole(multipliers), whole(couple)] + [pl.BlockSpec(memory_space=pl.ANY)] * len(previous),
            out_specs=[
                at((81, wide), 1), at((56, wide), 1), pl.BlockSpec((SUB, 5, 128, BLOCK), lambda i: (i + first, 0, 0, 0)),
            ],
            out_shape=[
                jax.ShapeDtypeStruct((81, pairs), F32),
                jax.ShapeDtypeStruct((56, pairs), F32),
                pltpu.HBM((blocks, 5, 128, BLOCK), F32),
            ],
            scratch_shapes=[
                pltpu.VMEM((SUB, 18, 128, BLOCK), F32),
                pltpu.VMEM((96, wide), F32),
                pltpu.VMEM((9, 16, wide), F32),
                pltpu.VMEM((64, segments), BF16),
            ],
            input_output_aliases={7 + i: i for i in range(len(previous))},
            compiler_params=vmem(28),
            cost_estimate=pl.CostEstimate(flops=10**9, transcendentals=0, bytes_accessed=15 * 10**6),
            name="terms",
        )(qs, qm, qw, sl, ml, multipliers, couple, *previous)

    done = terms_call(0, steps, ())
    column, (coupling, terms, quads) = lax.optimization_barrier((column, done))
    plane = from_chips(column)
    other = from_core(plane)
    quads = pltpu.with_memory_space_constraint(quads, pltpu.HBM)

    shape = (devices, 56, 128) if cap == 128 else (devices * cap // 256, 56, 256)
    outgoing = pl.pallas_call(
        functools.partial(slots_kernel, devices=devices, cap=cap),
        out_shape=jax.ShapeDtypeStruct(shape, F32),
        scratch_shapes=[pltpu.VMEM((112 * devices * cap // 256, pairs), BF16)],
        compiler_params=vmem(30),
        name="slots",
    )(owner, terms)
    if cap != 128:
        outgoing = outgoing.reshape(shape[0], 56, 256 // cap, cap).transpose(0, 2, 1, 3).reshape(devices, 56, cap)
    incoming = lax.all_to_all(outgoing, AXES, split_axis=0, concat_axis=0, tiled=True)
    if cap != 128:
        incoming = (
            incoming.reshape(devices * cap // 128, 128 // cap, 56, cap).transpose(0, 2, 1, 3).reshape(-1, 56, 128)
        )

    expand = jnp.asarray(expansion(), BF16)
    hbm = pl.BlockSpec(memory_space=pl.ANY)
    weighted_gap, slave_mass = pl.pallas_call(
        gap_kernel,
        grid=(steps,),
        in_specs=[
            pl.BlockSpec(memory_space=pltpu.SMEM), planes_spec, whole(sl), whole(ml),
            whole(slave_coords), whole(slave_disp), whole(slave_normals), whole(expand), hbm, hbm,
        ],
        out_specs=[pl.BlockSpec((9, segments), lambda i: (0, 0)), pl.BlockSpec((81, segments), lambda i: (0, 0))],
        out_shape=[jax.ShapeDtypeStruct((9, segments), F32), jax.ShapeDtypeStruct((81, segments), F32)],
        scratch_shapes=[
            pltpu.VMEM((devices * segments // 4, 128), F32),
            pltpu.VMEM((128, segments), BF16),
            pltpu.VMEM((48, segments), F32),
            pltpu.VMEM((48, pairs), F32),
            pltpu.VMEM((SUB, BLOCK, 128), F32),
            pltpu.VMEM((64, pairs), F32),
            pltpu.VMEM((SUB, 81, 8, BLOCK), F32),
            pltpu.VMEM((segments, pairs), BF16),
            pltpu.SemaphoreType.DMA((2,)),
        ],
        compiler_params=vmem(30),
        cost_estimate=pl.CostEstimate(flops=GAP_FLOPS, transcendentals=0, bytes_accessed=GAP_BYTES),
        name="gap",
    )(rows, quads, sl, ml, slave_coords, slave_disp, slave_normals, expand, plane, other)

    force, master_mass = pl.pallas_call(
        owner_kernel,
        out_shape=[jax.ShapeDtypeStruct((27, segments), F32), jax.ShapeDtypeStruct((81, segments), F32)],
        compiler_params=vmem(28),
        name="owner",
    )(incoming, expand)
    return coupling, weighted_gap, slave_mass, force, master_mass


def solution(mesh):
    split = P(AXES)
    table = P(None, None, AXES)
    return jax.shard_map(
        shards,
        mesh=mesh,
        in_specs=(
            split, P(AXES, None), split, P(AXES, None, None), P(AXES, None, None), P(AXES, None),
            table, table, table, table, table, table,
        ),
        out_specs=(P(None, AXES),) * 5,
        check_vma=False,
    )
```

```python
import functools

import jax
import jax.numpy as jnp
import numpy as np
from jax import lax
from jax.experimental import pallas as pl
from jax.experimental.pallas import tpu as pltpu
from jax.sharding import PartitionSpec as P

AXES = ("patch", "seg")
BLOCK = 128
SUB = 8
GAP_FLOPS = 2 * 10**9
GAP_BYTES = 60 * 10**6
UNROLL = (16, 16, 16)
F32 = jnp.float32
BF16 = jnp.bfloat16


LAGRANGE = np.array([(0, -0.5, 0.5), (1, 0, -1), (0, 0.5, 0.5)], np.float32)


def from_powers():
    nodes = np.einsum("jn,im->jinm", LAGRANGE, LAGRANGE).reshape(9, 9)
    table = np.zeros((88, 96), np.float32)
    for at, column in enumerate(np.einsum("ac,bd->cdab", nodes, nodes).reshape(81, 81)):
        table[:81, 32 * (at // 27) + at % 27] = column
    return np.concatenate([table, table], axis=1)


def power_products():
    return np.array([[np.convolve(p, q) for q in LAGRANGE] for p in LAGRANGE], np.float32)


def extra_moments():
    return [(m, n) for m in (3, 4) for n in range(5)] + [(m, n) for m in range(3) for n in (3, 4)]


def expansion():
    axis = power_products()
    table = np.zeros((81, 32), np.float32)
    columns = [(m, n) for n in range(3) for m in range(3)] + extra_moments()
    for b in range(9):
        for c in range(9):
            for at, (m, n) in enumerate(columns):
                table[9 * b + c, at] = axis[b % 3, c % 3, m] * axis[b // 3, c // 3, n]
    return table


def powers(t):
    square = t * t
    return [None, t, square, square * t, square * square]


def power_rows(x):
    def along(at, stride):
        out = [None] * 9
        for q in range(3):
            low, middle, high = (at[q * (4 - stride) + stride * i] for i in range(3))
            for i, block in enumerate((middle, 0.5 * (high - low), 0.5 * (high + low) - middle)):
                out[q * (4 - stride) + stride * i] = block
        return out

    return along(along(x, 1), 3)


def split2(x):
    high = x.astype(BF16)
    low = (x - high.astype(F32)).astype(BF16)
    return high, low


def stack2(x):
    high = x.astype(BF16).astype(F32)
    return jnp.concatenate([high, x - high], axis=0).astype(BF16)


def dot(a, b):
    return jnp.dot(a, b, preferred_element_type=F32)


def dot_nt(a, b):
    return lax.dot_general(a, b, (((1,), (1,)), ((), ())), preferred_element_type=F32)


def joined(product):
    half = product.shape[0] // 2
    return product[:half] + product[half:]


def one_hot(index_row, rows):
    at = lax.broadcasted_iota(jnp.int32, (rows, index_row.shape[1]), 0)
    return jnp.where(at == index_row, 1.0, 0.0).astype(BF16)


def total(x):
    return jnp.sum(x, axis=0, keepdims=True)


def merged(x, y, distance):
    rows = lax.broadcasted_iota(jnp.int32, (8, BLOCK), 0)
    first = (rows & distance) == 0
    if distance == 4:
        return jnp.where(first, x, y) + pltpu.roll(jnp.where(first, y, x), 4, 0)
    return jnp.where(first, x, y) + jnp.where(first, pltpu.roll(x, 8 - distance, 0), pltpu.roll(y, distance, 0))


def put_totals(ref, row, lanes, sums):
    for at in range(0, len(sums), 8):
        part = list(sums[at : at + 8])
        if len(part) == 1:
            ref[row + at : row + at + 1, lanes] = total(part[0])
            continue
        count = len(part)
        part = part + part[:1] * (8 - count)
        for distance in (4, 2, 1):
            part = [merged(part[k], part[k + distance], distance) for k in range(distance)]
        ref[row + at : row + at + count, lanes] = part[0][:count]


def planes(ref, sub):
    at = 2 * BLOCK * sub
    return ref[pl.ds(at, BLOCK, stride=2), :].T, ref[pl.ds(at + 1, BLOCK, stride=2), :].T


def product(*factors):
    value = None
    for x in factors:
        if x is not None:
            value = x if value is None else value * x
    return value


def extra_products(w, first, second):
    weighted = [product(w, x) for x in first]
    return [product(weighted[m], second[n]) for m, n in extra_moments()]


def accumulated(count, body, unroll):
    def step(c, sums):
        at = c * 8 if isinstance(c, int) else pl.multiple_of(c * 8, 8)
        return tuple(x + y for x, y in zip(sums, body(pl.ds(at, 8))))

    start = tuple(jnp.zeros((8, BLOCK), F32) for _ in range(count))
    return lax.fori_loop(0, 16, step, start, unroll=unroll)


def fill_rows(table_ref, start, blocks):
    half = table_ref.shape[0] // 2
    for a, block in enumerate(blocks):
        high, low = split2(block)
        at = start + 3 * a
        table_ref[at : at + 3, :] = high
        table_ref[at + half : at + half + 3, :] = low


def terms_kernel(qs_ref, qm_ref, w_ref, sl_ref, ml_ref, lam_ref, couple_ref, *rest):
    coupling_ref, terms_ref, planes_ref, shape_ref, c_ref, block_ref, lam_table_ref = rest[-7:]
    segments = lam_ref.shape[2]

    @pl.when(pl.program_id(0) == 0)
    def _():
        c_ref[...] = jnp.zeros_like(c_ref)
        fill_rows(lam_table_ref, 0, [lam_ref[a] for a in range(9)])

    for sub in range(SUB):
        w = w_ref[sub * BLOCK : (sub + 1) * BLOCK, :].T
        for at, plane in enumerate((*planes(qs_ref, sub), *planes(qm_ref, sub), w)):
            planes_ref[sub, at] = plane
    lam = joined(dot(lam_table_ref[...], one_hot(sl_ref[...], segments)))
    for sub in range(SUB):
        crossed_sums(sub, planes_ref, shape_ref, c_ref, terms_ref)
    moments = c_ref[...]
    coupling = dot(couple_ref[...], stack2(moments))
    coupling_ref[...] = coupling[0:81]
    for a in range(9):
        block_ref[a, 0:9, :] = coupling[9 * a : 9 * a + 9]
    for k in range(3):
        force = block_ref[0, 0:9, :] * lam[k : k + 1, :]
        for a in range(1, 9):
            force = force + block_ref[a, 0:9, :] * lam[3 * a + k : 3 * a + k + 1, :]
        terms_ref[9 * k : 9 * k + 9, :] = force
    terms_ref[27:36, :] = moments[0:9]
    terms_ref[52:53, :] = ml_ref[...].astype(F32)
    terms_ref[53:56, :] = jnp.zeros((3, SUB * BLOCK), F32)


def crossed_sums(sub, planes_ref, shape_ref, c_ref, terms_ref):
    lanes = slice(sub * BLOCK, (sub + 1) * BLOCK)

    def prepared(rows):
        s, t, u, v, w = (planes_ref[sub, at, rows, :] for at in range(5))
        fs, ft, fu, fv = powers(s), powers(t), powers(u), powers(v)
        for j in range(3):
            for i in range(3):
                if i + j > 0:
                    shape_ref[sub, 3 * j + i, rows, :] = product(fu[i], fv[j])
                shape_ref[sub, 9 + 3 * j + i, rows, :] = product(w, fs[i], ft[j])
        return extra_products(w, fu, fv)

    put_totals(terms_ref, 36, lanes, accumulated(16, prepared, UNROLL[0]))
    for j in range(3):

        def crossed(rows):
            master = [None] + [shape_ref[sub, b, rows, :] for b in range(1, 9)]
            slave = [shape_ref[sub, 9 + 3 * j + i, rows, :] for i in range(3)]
            return [product(x, y) for x in slave for y in master]

        put_totals(c_ref, 32 * j, lanes, accumulated(27, crossed, UNROLL[1]))


def slots_kernel(owner_ref, terms_ref, out_ref, left_ref, *, devices, cap):
    pairs = owner_ref.shape[1]
    width = 256
    per = width // cap
    groups = devices // per
    owner = owner_ref[...]
    upper = jnp.where(
        lax.broadcasted_iota(jnp.int32, (width, width), 0) < lax.broadcasted_iota(jnp.int32, (width, width), 1),
        1.0,
        0.0,
    ).astype(BF16)
    carry = jnp.zeros((devices, 1), F32)
    ranks = []
    for at in range(0, pairs, width):
        mine = one_hot(owner[:, at : at + width], devices)
        before = dot(mine, upper) + carry
        wide = mine.astype(F32)
        ranks.append(total(wide * before))
        carry = carry + jnp.sum(wide, axis=1, keepdims=True)
    rank = jnp.concatenate(ranks, axis=1).astype(jnp.int32)
    group = owner // per
    column = (owner - group * per) * cap + rank
    place = one_hot(column, width)
    both = stack2(terms_ref[...])
    rows = both.shape[0]
    for g in range(groups):
        left_ref[g * rows : (g + 1) * rows, :] = both * jnp.where(group == g, 1.0, 0.0).astype(BF16)
    sent = dot_nt(left_ref[...], place)
    for g in range(groups):
        block = joined(sent[g * rows : (g + 1) * rows])
        if cap == 128:
            out_ref[2 * g] = block[:, :128]
            out_ref[2 * g + 1] = block[:, 128:]
        else:
            out_ref[g] = block


def table_kernel(coords_ref, disp_ref, owner_ref, local_ref, out_ref, place_ref, rows_ref):
    place_ref[...] = relative_owner(owner_ref[...]) * out_ref.shape[0] + local_ref[...] % 128
    rows_ref[...] = jnp.zeros_like(rows_ref)
    for i, block in enumerate(power_rows([coords_ref[a] + disp_ref[a] for a in range(9)])):
        for c in range(block.shape[1] // 128):
            at = 32 * c + 3 * i
            rows_ref[at : at + 3, :] = block[:, 128 * c : 128 * (c + 1)]
    out_ref[...] = rows_ref[...].T


def gap_kernel(
    row_ref, planes_ref, sl_ref, ml_ref, coords_ref, disp_ref, normals_ref, expand_ref, near_ref, far_ref,
    gap_ref, mass_ref, table_ref, slave_ref, sums_ref, a_ref, picked_ref, coef_ref, wide_ref, hot_ref, sems,
):
    segments = coords_ref.shape[2]
    step = pl.program_id(0)

    @pl.when(step == 0)
    def _():
        half = near_ref.shape[0]
        copies = [
            pltpu.make_async_copy(near_ref, table_ref.at[pl.ds(0, half)], sems.at[0]),
            pltpu.make_async_copy(far_ref, table_ref.at[pl.ds(half, half)], sems.at[1]),
        ]
        for copy in copies:
            copy.start()
        a_ref[...] = jnp.zeros_like(a_ref)
        slave_ref[...] = jnp.zeros_like(slave_ref)
        fill_rows(slave_ref, 0, power_rows([coords_ref[a] + disp_ref[a] for a in range(9)]))
        fill_rows(slave_ref, 32, power_rows([normals_ref[a] for a in range(9)]))
        hot_ref[...] = one_hot(sl_ref[...], segments)
        coef_ref[0:64, :] = joined(dot(slave_ref[...], hot_ref[...]))
        for copy in copies:
            copy.wait()

    for sub in range(SUB):
        gap_block(sub, step, row_ref, ml_ref, planes_ref, table_ref, picked_ref, coef_ref, wide_ref, a_ref, segments)

    @pl.when(step == pl.num_programs(0) - 1)
    def _():
        sums_ref[...] = joined(dot_nt(stack2(a_ref[...]), hot_ref[...]))
        for j in range(3):
            for i in range(3):
                row = None
                for m, n, sign in lagrange_terms(i, j):
                    part = sums_ref[32 + 3 * n + m : 33 + 3 * n + m, :] * sign
                    row = part if row is None else row + part
                gap_ref[3 * j + i : 3 * j + i + 1, :] = row
        mass_ref[...] = expanded(expand_ref[...], sums_ref[0:32, :])


def gap_block(sub, step, row_ref, ml_ref, planes_ref, table_ref, picked_ref, coef_ref, wide_ref, a_ref, segments):
    start = pl.multiple_of((step * SUB + sub) * BLOCK, BLOCK)
    for p in range(BLOCK):
        picked_ref[sub, p : p + 1, :] = table_ref[pl.ds(row_ref[0, start + p], 1), :]
    picked = picked_ref[sub].T
    quarter = ml_ref[:, pl.ds(start, BLOCK)] // 128
    position = picked[0:32]
    for c in range(1, segments // 128):
        position = jnp.where(quarter == c, picked[32 * c : 32 * c + 32], position)
    here = pl.ds(start, BLOCK)
    for row in range(54):
        at = row if row < 27 else row + 5
        wide_ref[sub, row] = jnp.broadcast_to(coef_ref[at : at + 1, here], (8, BLOCK))
    for row in range(27):
        wide_ref[sub, 54 + row] = jnp.broadcast_to(position[row : row + 1], (8, BLOCK))

    def field(row, first, second):
        value = None
        for j in range(3):
            c = [wide_ref[sub, row + 9 * j + 3 * i] for i in range(3)]
            part = c[0] + c[1] * first[1] + c[2] * first[2]
            value = part if j == 0 else value + part * second[j]
        return value

    def moments(rows):
        s, t, u, v, w = (planes_ref[sub, at, rows, :] for at in range(5))
        fs, ft, fu, fv = powers(s), powers(t), powers(u), powers(v)
        gap = None
        for k in range(3):
            part = field(27 + k, fs, ft) * (field(54 + k, fu, fv) - field(k, fs, ft))
            gap = part if gap is None else gap + part
        base = [product(w, m, n) for n in ft[:3] for m in fs[:3]]
        return base + extra_products(w, fs, ft) + [x * gap for x in base]

    sums = accumulated(34, moments, UNROLL[2])
    put_totals(a_ref, 0, here, sums[:25])
    put_totals(a_ref, 32, here, sums[25:])


def lagrange_terms(i, j):
    axis = {0: [(1, -0.5), (2, 0.5)], 1: [(0, 1.0), (2, -1.0)], 2: [(1, 0.5), (2, 0.5)]}
    return [(m, n, p * q) for m, p in axis[i] for n, q in axis[j]]


def expanded(table, moments):
    high = moments.astype(BF16)
    rest = moments - high.astype(F32)
    middle = rest.astype(BF16)
    low = (rest - middle.astype(F32)).astype(BF16)
    return dot(table, high) + dot(table, middle) + dot(table, low)


def owner_kernel(in_ref, expand_ref, force_ref, mass_ref):
    chunks = in_ref.shape[0]
    segments = force_ref.shape[1]
    rows = 2 * in_ref.shape[1]
    half = segments // 2
    sums = jnp.zeros((2 * rows, half), F32)
    for at in range(0, chunks, 2):
        terms = jnp.concatenate([in_ref[at], in_ref[at + 1]], axis=1)
        local = terms[52:53, :].astype(jnp.int32)
        both = stack2(terms)
        upper = jnp.where(local >= half, 1.0, 0.0).astype(BF16)
        left = jnp.concatenate([both * (1 - upper), both * upper], axis=0)
        sums = sums + dot_nt(left, one_hot(local % half, half))
    sums = jnp.concatenate([sums[:rows], sums[rows:]], axis=1)
    sums = joined(sums)
    force_ref[...] = sums[0:27, :]
    moments = jnp.concatenate([sums[27:52, :], jnp.zeros((7, segments), F32)], axis=0)
    mass_ref[...] = expanded(expand_ref[...], moments)


def vmem(mib):
    return pltpu.CompilerParams(vmem_limit_bytes=mib << 20)


def from_patches(block):
    patches = lax.axis_size("patch")
    parts = [block]
    for d in range(1, patches):
        parts.append(lax.ppermute(block, "patch", [((i + d) % patches, i) for i in range(patches)]))
    return jnp.concatenate(parts, axis=0)


def from_chips(column):
    segs = lax.axis_size("seg")
    parts = [column]
    for d in range(1, segs // 2):
        parts.append(lax.ppermute(column, "seg", [(i ^ (2 * d), i) for i in range(segs)]))
    return jnp.concatenate(lax.optimization_barrier(parts), axis=0)


def from_core(plane):
    return lax.ppermute(plane, "seg", [(i ^ 1, i) for i in range(lax.axis_size("seg"))])


def relative_owner(owner):
    patches, segs = lax.axis_size("patch"), lax.axis_size("seg")
    mine = lax.axis_index("seg")
    patch = jnp.mod(owner // segs - lax.axis_index("patch") + patches, patches)
    seg = jnp.bitwise_xor(owner % segs, mine)
    return (seg % 2) * (patches * segs // 2) + (seg // 2) * patches + patch


def shards(
    slave_local,
    owner_route,
    master_local,
    quad_slave,
    quad_master,
    quad_weight,
    slave_coords,
    slave_disp,
    slave_normals,
    multipliers,
    master_coords,
    master_disp,
):
    pairs = slave_local.shape[0]
    segments = slave_coords.shape[2]
    devices = lax.axis_size(AXES)
    cap = 2 * pairs // devices
    blocks = pairs // BLOCK
    steps = blocks // SUB
    wide = SUB * BLOCK

    slave_coords, slave_disp, slave_normals, multipliers, master_coords, master_disp = (
        pltpu.with_memory_space_constraint(jnp.transpose(x, (1, 0, 2)), pltpu.HBM)
        for x in (slave_coords, slave_disp, slave_normals, multipliers, master_coords, master_disp)
    )
    qs, qm, qw, sl, ml, owner = (
        pltpu.with_memory_space_constraint(x, pltpu.HBM)
        for x in (
            quad_slave.reshape(2 * pairs, 128),
            quad_master.reshape(2 * pairs, 128),
            quad_weight,
            slave_local.reshape(1, pairs),
            master_local.reshape(1, pairs),
            owner_route.reshape(1, pairs),
        )
    )
    block, rows = pl.pallas_call(
        table_kernel,
        out_shape=[jax.ShapeDtypeStruct((segments // 4, 128), F32), jax.ShapeDtypeStruct((1, pairs), jnp.int32)],
        scratch_shapes=[pltpu.VMEM((128, segments // 4), F32)],
        name="table",
    )(master_coords, master_disp, owner, ml)
    column = from_patches(block)

    planes_spec = pl.BlockSpec((SUB, 5, 128, BLOCK), lambda i: (i, 0, 0, 0))
    row_spec = pl.BlockSpec((1, wide), lambda i: (0, i))

    def whole(x):
        return pl.BlockSpec(x.shape, lambda i: (0,) * len(x.shape))

    couple = pltpu.with_memory_space_constraint(jnp.asarray(from_powers(), BF16), pltpu.HBM)

    def terms_call(first, last, previous):

        def at(spec, dim):
            return pl.BlockSpec(spec, lambda i: tuple(i + first if d == dim else 0 for d in range(2)))

        weight = at((wide, 128), 0)
        quad = at((2 * wide, 128), 0)
        row = at((1, wide), 1)
        return pl.pallas_call(
            terms_kernel,
            grid=(last - first,),
            in_specs=[quad, quad, weight, row, row, whole(multipliers), whole(couple)] + [pl.BlockSpec(memory_space=pl.ANY)] * len(previous),
            out_specs=[
                at((81, wide), 1), at((56, wide), 1), pl.BlockSpec((SUB, 5, 128, BLOCK), lambda i: (i + first, 0, 0, 0)),
            ],
            out_shape=[
                jax.ShapeDtypeStruct((81, pairs), F32),
                jax.ShapeDtypeStruct((56, pairs), F32),
                pltpu.HBM((blocks, 5, 128, BLOCK), F32),
            ],
            scratch_shapes=[
                pltpu.VMEM((SUB, 18, 128, BLOCK), F32),
                pltpu.VMEM((96, wide), F32),
                pltpu.VMEM((9, 16, wide), F32),
                pltpu.VMEM((64, segments), BF16),
            ],
            input_output_aliases={7 + i: i for i in range(len(previous))},
            compiler_params=vmem(48),
            cost_estimate=pl.CostEstimate(flops=10**9, transcendentals=0, bytes_accessed=15 * 10**6),
            name="terms",
        )(qs, qm, qw, sl, ml, multipliers, couple, *previous)

    done = terms_call(0, steps, ())
    column, (coupling, terms, quads) = lax.optimization_barrier((column, done))
    plane = from_chips(column)
    other = from_core(plane)
    quads = pltpu.with_memory_space_constraint(quads, pltpu.HBM)

    shape = (devices, 56, 128) if cap == 128 else (devices * cap // 256, 56, 256)
    outgoing = pl.pallas_call(
        functools.partial(slots_kernel, devices=devices, cap=cap),
        out_shape=jax.ShapeDtypeStruct(shape, F32),
        scratch_shapes=[pltpu.VMEM((112 * devices * cap // 256, pairs), BF16)],
        compiler_params=vmem(48),
        name="slots",
    )(owner, terms)
    if cap != 128:
        outgoing = outgoing.reshape(shape[0], 56, 256 // cap, cap).transpose(0, 2, 1, 3).reshape(devices, 56, cap)
    incoming = lax.all_to_all(outgoing, AXES, split_axis=0, concat_axis=0, tiled=True)
    if cap != 128:
        incoming = (
            incoming.reshape(devices * cap // 128, 128 // cap, 56, cap).transpose(0, 2, 1, 3).reshape(-1, 56, 128)
        )

    expand = jnp.asarray(expansion(), BF16)
    hbm = pl.BlockSpec(memory_space=pl.ANY)
    weighted_gap, slave_mass = pl.pallas_call(
        gap_kernel,
        grid=(steps,),
        in_specs=[
            pl.BlockSpec(memory_space=pltpu.SMEM), planes_spec, whole(sl), whole(ml),
            whole(slave_coords), whole(slave_disp), whole(slave_normals), whole(expand), hbm, hbm,
        ],
        out_specs=[pl.BlockSpec((9, segments), lambda i: (0, 0)), pl.BlockSpec((81, segments), lambda i: (0, 0))],
        out_shape=[jax.ShapeDtypeStruct((9, segments), F32), jax.ShapeDtypeStruct((81, segments), F32)],
        scratch_shapes=[
            pltpu.VMEM((devices * segments // 4, 128), F32),
            pltpu.VMEM((128, segments), BF16),
            pltpu.VMEM((48, segments), F32),
            pltpu.VMEM((48, pairs), F32),
            pltpu.VMEM((SUB, BLOCK, 128), F32),
            pltpu.VMEM((64, pairs), F32),
            pltpu.VMEM((SUB, 81, 8, BLOCK), F32),
            pltpu.VMEM((segments, pairs), BF16),
            pltpu.SemaphoreType.DMA((2,)),
        ],
        compiler_params=vmem(48),
        cost_estimate=pl.CostEstimate(flops=GAP_FLOPS, transcendentals=0, bytes_accessed=GAP_BYTES),
        name="gap",
    )(rows, quads, sl, ml, slave_coords, slave_disp, slave_normals, expand, plane, other)

    force, master_mass = pl.pallas_call(
        owner_kernel,
        out_shape=[jax.ShapeDtypeStruct((27, segments), F32), jax.ShapeDtypeStruct((81, segments), F32)],
        compiler_params=vmem(48),
        name="owner",
    )(incoming, expand)
    return coupling, weighted_gap, slave_mass, force, master_mass


def solution(mesh):
    split = P(AXES)
    table = P(None, None, AXES)
    return jax.shard_map(
        shards,
        mesh=mesh,
        in_specs=(
            split, P(AXES, None), split, P(AXES, None, None), P(AXES, None, None), P(AXES, None),
            table, table, table, table, table, table,
        ),
        out_specs=(P(None, AXES),) * 5,
        check_vma=False,
    )
```
